512 devices in a mesh: sec: 8 (over z_lo, x), gx: 16 (over y, core), gy: 4 (over z_hi).
Axes of the slice: x: 4, y: 8, z: 8 (z_hi: 4, z_lo: 2; z = z_hi * 2 + z_lo), core: 2. Of those that a mesh axis runs over, the one named last changes fastest.
Arguments:
- fields: float32 [8, 5, 512, 1024], P('sec', None, 'gx', 'gy'), may hold values from -1.5 to 6, as said below
- stored_rates: bfloat16 [8, 3, 5, 512, 1024], P('sec', None, None, 'gx', 'gy'), may hold values from -6 to 6
Outputs:
- advanced: float32 [8, 5, 512, 1024], P('sec', None, 'gx', 'gy')
The draws below stay inside these ranges and needn't reach their ends.
Inputs may be any that keep to these rules, and one draw needn't show every extreme that they name: `fields`: for every level and cell: density in [0.6, 1.4], every velocity component within 0.9 in magnitude, pressure in [0.6, 1.4]; momenta are density times velocity and energy is pressure / 0.4 plus density times kinetic energy.
All inputs are finite; a program needn't handle non-finite values.
Results may differ from the reference program's by a relative error of at most 0.0005.
Values may be sent and summed in bfloat16 or wider, within the bound.
A program may use at most 64 MiB of HBM per device.

```python
import jax
import jax.numpy as jnp

NZ = 32
TICKS = 3
LEVELS = 4
MEMBERS = 2
NX = 512
NY = 32


def draw_fields(key, part):
    keys = jax.random.split(jax.random.fold_in(key, 17), 3)
    shape = (MEMBERS * LEVELS, NX, NY * NZ)
    matter_per_volume = jax.random.uniform(keys[0], shape, jnp.float32, 0.7, 1.3)
    velocity = jnp.clip(0.45 * jax.random.normal(keys[1], (3,) + shape, jnp.float32), -0.9, 0.9)
    normal_stress_scalar = jax.random.uniform(keys[2], shape, jnp.float32, 0.6, 1.4)
    motion_half_square = 0.5 * (velocity[0] * velocity[0] + velocity[1] * velocity[1] + velocity[2] * velocity[2])
    energy = normal_stress_scalar / 0.4 + matter_per_volume * motion_half_square
    return jnp.stack([matter_per_volume, matter_per_volume * velocity[0], matter_per_volume * velocity[1], matter_per_volume * velocity[2], energy], axis=1)


def shard_levels(key, shape, shards, smallest, top_value):
    gain, own = 1.0, jax.random.fold_in(key, 6)
    for position, parts in shards:
        heights = jnp.exp(jax.random.uniform(jax.random.fold_in(own, position), (parts,), jnp.float32, smallest / len(shards), top_value / len(shards)))
        gain = gain * jnp.repeat(heights, shape[position] // parts).reshape([-1 if axis == position else 1 for axis in range(len(shape))])
    return gain


def scatter_about(own_key, shape, spread, reach, pieces=(), dtype=jnp.bfloat16):
    level = shard_levels(own_key, shape, pieces, -0.22, 0.18) if pieces else 1.0
    drawn = jax.random.normal(own_key, shape, jnp.float32) * spread * level
    return jnp.minimum(jnp.maximum(drawn, -reach), reach).astype(dtype)


def setup_inputs(seed: int = 0) -> dict:
    arg_keys = jax.random.split(jax.random.key(seed), 3)
    return {
        "fields": draw_fields(jax.random.fold_in(arg_keys[2], 71), 0),
        "stored_rates": scatter_about(arg_keys[1], (MEMBERS * LEVELS, 3, 5, NX, NY * NZ), 1.0, 6.0, ((0, 8), (3, 16), (4, 4))),
    }


TIME_STEP = 0.04
DYNAMIC_FRICTION = 0.4
CONDUCTIVITY = 0.5
GAMMA_LESS = 0.4
QUAD_WEIGHTS = (1.0 / 24.0, -5.0 / 24.0, 19.0 / 24.0, 9.0 / 24.0)


def shift_z(values, step, depth):
    column = jax.lax.broadcasted_iota(jnp.int32, values.shape, values.ndim - 1) % depth
    unwrapped = jnp.roll(values, -step, axis=-1)
    if step > 0:
        wrapped = jnp.roll(values, depth - step, axis=-1)
        inside = column + step < depth
    else:
        wrapped = jnp.roll(values, -step - depth, axis=-1)
        inside = column + step >= 0
    return jnp.where(inside, unwrapped, wrapped)


def rates(matter_per_volume, mom_x, mom_y, mom_z, energy, window, depth):
    vel_x = mom_x / matter_per_volume
    vel_y = mom_y / matter_per_volume
    vel_z = mom_z / matter_per_volume
    motion_half_square = 0.5 * (vel_x * vel_x + vel_y * vel_y + vel_z * vel_z)
    normal_stress_scalar = GAMMA_LESS * (energy - matter_per_volume * motion_half_square)
    gas_warmth_field = normal_stress_scalar / matter_per_volume
    enthalpy = energy + normal_stress_scalar

    def diff_x(values):
        return (window(values, 1, 0) - window(values, -1, 0)) * 0.5

    def diff_y(values):
        return (window(values, 0, 1) - window(values, 0, -1)) * 0.5

    def diff_z(values):
        center = window(values, 0, 0)
        return (shift_z(center, 1, depth) - shift_z(center, -1, depth)) * 0.5

    def middle_sweep_tier(values):
        center = window(values, 0, 0)
        along_x = window(values, 2, 0) - 2.0 * center + window(values, -2, 0)
        along_y = window(values, 0, 2) - 2.0 * center + window(values, 0, -2)
        along_z = shift_z(center, 2, depth) - 2.0 * center + shift_z(center, -2, depth)
        return (along_x + along_y + along_z) * 0.25

    mass = -(diff_x(mom_x) + diff_y(mom_y) + diff_z(mom_z))
    flow_x = -(diff_x(mom_x * vel_x + normal_stress_scalar) + diff_y(mom_x * vel_y) + diff_z(mom_x * vel_z)) + DYNAMIC_FRICTION * middle_sweep_tier(vel_x)
    flow_y = -(diff_x(mom_y * vel_x) + diff_y(mom_y * vel_y + normal_stress_scalar) + diff_z(mom_y * vel_z)) + DYNAMIC_FRICTION * middle_sweep_tier(vel_y)
    flow_z = -(diff_x(mom_z * vel_x) + diff_y(mom_z * vel_y) + diff_z(mom_z * vel_z + normal_stress_scalar)) + DYNAMIC_FRICTION * middle_sweep_tier(vel_z)
    conducted_warmth_current = -(diff_x(enthalpy * vel_x) + diff_y(enthalpy * vel_y) + diff_z(enthalpy * vel_z))
    conducted_warmth_current = conducted_warmth_current + DYNAMIC_FRICTION * middle_sweep_tier(motion_half_square) + CONDUCTIVITY * middle_sweep_tier(gas_warmth_field)
    return jnp.stack([mass, flow_x, flow_y, flow_z, conducted_warmth_current])


def level_rates(level_state):
    def window(values, across, along):
        return jnp.roll(values, (-across, -along * NZ), (0, 1))

    return rates(level_state[0], level_state[1], level_state[2], level_state[3], level_state[4], window, NZ)


def advance_member(member_fields, member_stored):
    levels = member_fields.shape[0]
    current = member_fields
    stored = member_stored
    first_level = (jnp.arange(levels) == 0)[:, None, None, None]
    for tick_count in range(TICKS):
        own_rates = jnp.stack([level_rates(current[level]) for level in range(levels)])
        lower = own_rates[:-1].astype(jnp.bfloat16)
        fresh_rates = jnp.concatenate([jnp.zeros_like(lower[:1]), lower], axis=0)
        quadrature = (QUAD_WEIGHTS[0] * stored[:, 0].astype(jnp.float32)
                      + QUAD_WEIGHTS[1] * stored[:, 1].astype(jnp.float32)
                      + QUAD_WEIGHTS[2] * stored[:, 2].astype(jnp.float32)
                      + QUAD_WEIGHTS[3] * fresh_rates.astype(jnp.float32))
        correction = quadrature - stored[:, 2].astype(jnp.float32)
        current = current + TIME_STEP * (own_rates + jnp.where(first_level, jnp.float32(0.0), correction))
        stored = jnp.concatenate([stored[:, 1:], fresh_rates[:, None]], axis=1)
    return current


def reference(fields, stored_rates):
    results = []
    for member in range(MEMBERS):
        start = member * LEVELS
        results.append(advance_member(fields[start:start + LEVELS], stored_rates[start:start + LEVELS]))
    return jnp.concatenate(results, axis=0)
```

```python
import jax
import jax.numpy as jnp
from jax import lax
from jax.experimental import pallas as pl
from jax.experimental.pallas import tpu as pltpu
from jax.sharding import PartitionSpec as P

NZ = 32
TICKS = 3
LEVELS = 4
TIME_STEP = 0.04
DYNAMIC_FRICTION = 0.4
CONDUCTIVITY = 0.5
GAMMA_LESS = 0.4
W0, W1, W2, W3 = 1.0 / 24.0, -5.0 / 24.0, 19.0 / 24.0 - 1.0, 9.0 / 24.0
MESH = pl.DeviceIdType.MESH


def primitives(density, mom_x, mom_y, mom_z, energy):
    inverse = 1.0 / density
    vel = (mom_x * inverse, mom_y * inverse, mom_z * inverse)
    kinetic = 0.5 * (vel[0] * vel[0] + vel[1] * vel[1] + vel[2] * vel[2])
    pressure = GAMMA_LESS * (energy - density * kinetic)
    heat = DYNAMIC_FRICTION * kinetic + CONDUCTIVITY * (pressure * inverse)
    return (mom_x, mom_y, mom_z), vel, pressure, energy + pressure, heat


def flux_difference(axis, prims, difference):
    mom, vel, pressure, enthalpy, heat = prims
    terms = [difference(mom[axis]) * -0.5]
    for c in range(3):
        flux = mom[c] * vel[axis]
        if c == axis:
            flux = flux + pressure
        spread = difference(vel[c]) * (0.5 * DYNAMIC_FRICTION)
        terms.append(difference(spread - flux) * 0.5)
    spread = difference(heat) * 0.5
    terms.append(difference(spread - enthalpy * vel[axis]) * 0.5)
    return terms


def ring_difference(axis, step):
    def difference(values):
        size = values.shape[axis]
        return pltpu.roll(values, size - step, axis) - pltpu.roll(values, step, axis)

    return difference


def z_difference(values):
    lane = lax.broadcasted_iota(jnp.int32, values.shape, 1) % NZ
    up = jnp.where(
        lane < NZ - 1, pltpu.roll(values, 127, 1), pltpu.roll(values, NZ - 1, 1)
    )
    down = jnp.where(lane > 0, pltpu.roll(values, 1, 1), pltpu.roll(values, 129 - NZ, 1))
    return up - down


def tree_concat(first, second, axis):
    return jax.tree.map(lambda a, b: jnp.concatenate([a, b], axis=axis), first, second)


def kernel(
    counts, fields, stored, out, u, st, rate, x_lo, x_hi, y_send, y_lo, y_hi,
    f_send, f_recv, load_sem, x_ss, x_rs, y_ss, y_rs, f_ss, f_rs,
):
    n_sec, n_gx, n_gy = counts
    sec, gx, gy = lax.axis_index("sec"), lax.axis_index("gx"), lax.axis_index("gy")
    level = lax.rem(sec, LEVELS)
    gx_up, gx_down = lax.rem(gx + 1, n_gx), lax.rem(gx + n_gx - 1, n_gx)
    gy_up, gy_down = lax.rem(gy + 1, n_gy), lax.rem(gy + n_gy - 1, n_gy)
    sec_up, sec_down = lax.rem(sec + 1, n_sec), lax.rem(sec + n_sec - 1, n_sec)
    has_up, has_down = level < LEVELS - 1, level > 0

    load_u = pltpu.make_async_copy(fields.at[0], u.at[0], load_sem.at[0])
    load_st = pltpu.make_async_copy(stored.at[0], st, load_sem.at[1])
    load_u.start()
    load_st.start()

    barrier = pltpu.get_barrier_semaphore()
    for target in ({"gx": gx_up}, {"gx": gx_down}, {"gy": gy_up}, {"gy": gy_down}):
        pl.semaphore_signal(barrier, inc=1, device_id=target, device_id_type=MESH)

    @pl.when(has_up)
    def _():
        pl.semaphore_signal(barrier, inc=1, device_id={"sec": sec_up}, device_id_type=MESH)

    @pl.when(has_down)
    def _():
        pl.semaphore_signal(barrier, inc=1, device_id={"sec": sec_down}, device_id_type=MESH)

    load_u.wait()

    def remote(src, dst, send, recv, target):
        return pltpu.make_async_remote_copy(
            src_ref=src, dst_ref=dst, send_sem=send, recv_sem=recv,
            device_id=target, device_id_type=MESH,
        )

    lane = lax.broadcasted_iota(jnp.int32, (16, 128), 1)
    row = lax.broadcasted_iota(jnp.int32, (8, 256), 0)
    copies = []
    for tick in range(TICKS):
        now = u.at[tick]
        for f in range(5):
            first, last = now[f, :, 0:128], now[f, :, 128:256]
            y_send[tick, 0, f] = jnp.where(
                lane < 64, first[0:16], pltpu.roll(first[16:32], 64, 1)
            ).astype(jnp.bfloat16)
            y_send[tick, 1, f] = jnp.where(
                lane < 64, pltpu.roll(last[16:32], 64, 1), last[0:16]
            ).astype(jnp.bfloat16)
        if tick == 0:
            pl.semaphore_wait(
                barrier, 4 + has_up.astype(jnp.int32) + has_down.astype(jnp.int32)
            )
        to_y = (
            remote(y_send.at[tick, 0], y_hi.at[tick], y_ss.at[tick, 0], y_rs.at[tick, 0], {"gy": gy_down}),
            remote(y_send.at[tick, 1], y_lo.at[tick], y_ss.at[tick, 1], y_rs.at[tick, 1], {"gy": gy_up}),
        )
        to_x = (
            remote(now.at[:, 0:8], x_hi.at[tick], x_ss.at[tick, 0], x_rs.at[tick, 0], {"gx": gx_down}),
            remote(now.at[:, 24:32], x_lo.at[tick], x_ss.at[tick, 1], x_rs.at[tick, 1], {"gx": gx_up}),
        )
        for copy in to_y + to_x:
            copy.start()
        copies += to_y + to_x

        for half in range(2):
            cols = slice(128 * half, 128 * half + 128)
            prims = primitives(*(now[f, :, cols] for f in range(5)))
            for f, term in enumerate(flux_difference(2, prims, z_difference)):
                rate[f, :, cols] = term

        main = primitives(*(now[f] for f in range(5)))
        for copy in to_x:
            copy.wait_recv()
        halo = primitives(
            *(jnp.where(row < 4, x_hi[tick, f], x_lo[tick, f]) for f in range(5))
        )
        ring = tree_concat(main, halo, 0)
        for f, term in enumerate(flux_difference(0, ring, ring_difference(0, 1))):
            rate[f] += term[0:32]

        for copy in to_y:
            copy.wait_recv()
        sides = []
        for f in range(5):
            high = y_hi[tick, f].astype(jnp.float32)
            low = y_lo[tick, f].astype(jnp.float32)
            top = jnp.where(lane < 64, high, low)
            bottom = pltpu.roll(jnp.where(lane < 64, low, high), 64, 1)
            sides.append(jnp.concatenate([top, bottom], axis=0))
        ring = tree_concat(main, primitives(*sides), 1)
        terms = flux_difference(1, ring, ring_difference(1, NZ))
        for f, term in enumerate(terms):
            own = rate[f] + term[:, 0:256]
            rate[f] = own
            f_send[tick, f] = own.astype(jnp.bfloat16)

        to_next = remote(
            f_send.at[tick], f_recv.at[tick], f_ss.at[tick], f_rs.at[tick], {"sec": sec_up}
        )

        @pl.when(has_up)
        def _():
            to_next.start()

        if tick == 0:
            load_st.wait()
        target = out.at[0] if tick == TICKS - 1 else u.at[tick + 1]

        @pl.when(level == 0)
        def _():
            for f in range(5):
                target[f] = now[f] + TIME_STEP * rate[f]

        @pl.when(has_down)
        def _():
            history = [st.at[h] for h in range(3)] + [f_recv.at[h] for h in range(tick)]
            a, b, c = history[tick : tick + 3]
            for f in range(5):
                known = (
                    W0 * a[f].astype(jnp.float32)
                    + W1 * b[f].astype(jnp.float32)
                    + W2 * c[f].astype(jnp.float32)
                )
                rate[f] = now[f] + TIME_STEP * (rate[f] + known)
            to_next.wait_recv()
            for f in range(5):
                target[f] = rate[f] + (TIME_STEP * W3) * f_recv[tick, f].astype(jnp.float32)

        @pl.when(has_up)
        def _():
            to_next.wait_send()

    for copy in copies:
        copy.wait_send()


def solution(mesh):
    counts = tuple(mesh.shape[name] for name in ("sec", "gx", "gy"))

    def per_device(fields, stored_rates):
        _, _, rows, cols = fields.shape
        halo_x = pltpu.VMEM((TICKS, 5, 8, cols), jnp.float32)
        halo_y = pltpu.VMEM((TICKS, 5, rows // 2, 128), jnp.bfloat16)
        block = (5, rows, cols)
        return pl.pallas_call(
            lambda *refs: kernel(counts, *refs),
            name="correct",
            out_shape=jax.ShapeDtypeStruct(fields.shape, fields.dtype),
            in_specs=[pl.BlockSpec(memory_space=pl.ANY)] * 2,
            out_specs=pl.BlockSpec(memory_space=pltpu.VMEM),
            scratch_shapes=[
                pltpu.VMEM((TICKS,) + block, jnp.float32),
                pltpu.VMEM((3,) + block, jnp.bfloat16),
                pltpu.VMEM(block, jnp.float32),
                halo_x,
                halo_x,
                pltpu.VMEM((TICKS, 2, 5, rows // 2, 128), jnp.bfloat16),
                halo_y,
                halo_y,
                pltpu.VMEM((TICKS,) + block, jnp.bfloat16),
                pltpu.VMEM((TICKS,) + block, jnp.bfloat16),
                pltpu.SemaphoreType.DMA((2,)),
                pltpu.SemaphoreType.DMA((TICKS, 2)),
                pltpu.SemaphoreType.DMA((TICKS, 2)),
                pltpu.SemaphoreType.DMA((TICKS, 2)),
                pltpu.SemaphoreType.DMA((TICKS, 2)),
                pltpu.SemaphoreType.DMA((TICKS,)),
                pltpu.SemaphoreType.DMA((TICKS,)),
            ],
            compiler_params=pltpu.CompilerParams(collective_id=0, has_side_effects=True),
        )(fields, stored_rates)

    return jax.shard_map(
        per_device,
        mesh=mesh,
        in_specs=(P("sec", None, "gx", "gy"), P("sec", None, None, "gx", "gy")),
        out_specs=P("sec", None, "gx", "gy"),
        check_vma=False,
    )
```

```python
import jax
import jax.numpy as jnp
from jax import lax
from jax.experimental import pallas as pl
from jax.experimental.pallas import tpu as pltpu
from jax.sharding import PartitionSpec as P

NZ = 32
TICKS = 3
LEVELS = 4
TIME_STEP = 0.04
DYNAMIC_FRICTION = 0.4
CONDUCTIVITY = 0.5
GAMMA_LESS = 0.4
W0, W1, W2, W3 = 1.0 / 24.0, -5.0 / 24.0, 19.0 / 24.0 - 1.0, 9.0 / 24.0
MESH = pl.DeviceIdType.MESH


def primitives(density, mom_x, mom_y, mom_z, energy):
    inverse = 1.0 / density
    vel = (mom_x * inverse, mom_y * inverse, mom_z * inverse)
    kinetic = 0.5 * (vel[0] * vel[0] + vel[1] * vel[1] + vel[2] * vel[2])
    pressure = GAMMA_LESS * (energy - density * kinetic)
    heat = DYNAMIC_FRICTION * kinetic + CONDUCTIVITY * (pressure * inverse)
    return (mom_x, mom_y, mom_z), vel, pressure, energy + pressure, heat


def flux_difference(axis, prims, difference):
    mom, vel, pressure, enthalpy, heat = prims
    terms = [difference(mom[axis]) * -0.5]
    for c in range(3):
        flux = mom[c] * vel[axis]
        if c == axis:
            flux = flux + pressure
        spread = difference(vel[c]) * (0.5 * DYNAMIC_FRICTION)
        terms.append(difference(spread - flux) * 0.5)
    spread = difference(heat) * 0.5
    terms.append(difference(spread - enthalpy * vel[axis]) * 0.5)
    return terms


def ring_difference(axis, step):
    def difference(values):
        size = values.shape[axis]
        return pltpu.roll(values, size - step, axis) - pltpu.roll(values, step, axis)

    return difference


def z_difference(values):
    lane = lax.broadcasted_iota(jnp.int32, values.shape, 1) % NZ
    up = jnp.where(
        lane < NZ - 1, pltpu.roll(values, 127, 1), pltpu.roll(values, NZ - 1, 1)
    )
    down = jnp.where(lane > 0, pltpu.roll(values, 1, 1), pltpu.roll(values, 129 - NZ, 1))
    return up - down


def tree_concat(first, second, axis):
    return jax.tree.map(lambda a, b: jnp.concatenate([a, b], axis=axis), first, second)


def kernel(
    counts, fields, stored, out, u, st, rate, inside, x_lo, x_hi, y_send, y_lo, y_hi,
    f_send, f_recv, load_sem, x_ss, x_rs, y_ss, y_rs, f_ss, f_rs,
):
    n_sec, n_gx, n_gy = counts
    sec, gx, gy = lax.axis_index("sec"), lax.axis_index("gx"), lax.axis_index("gy")
    level = lax.rem(sec, LEVELS)
    gx_up, gx_down = lax.rem(gx + 1, n_gx), lax.rem(gx + n_gx - 1, n_gx)
    gy_up, gy_down = lax.rem(gy + 1, n_gy), lax.rem(gy + n_gy - 1, n_gy)
    sec_up, sec_down = lax.rem(sec + 1, n_sec), lax.rem(sec + n_sec - 1, n_sec)
    has_up, has_down = level < LEVELS - 1, level > 0

    load_u = pltpu.make_async_copy(fields.at[0], u.at[0], load_sem.at[0])
    load_st = pltpu.make_async_copy(stored.at[0], st, load_sem.at[1])
    load_u.start()
    load_st.start()

    barrier = pltpu.get_barrier_semaphore()
    for target in ({"gx": gx_up}, {"gx": gx_down}, {"gy": gy_up}, {"gy": gy_down}):
        pl.semaphore_signal(barrier, inc=1, device_id=target, device_id_type=MESH)

    @pl.when(has_up)
    def _():
        pl.semaphore_signal(barrier, inc=1, device_id={"sec": sec_up}, device_id_type=MESH)

    @pl.when(has_down)
    def _():
        pl.semaphore_signal(barrier, inc=1, device_id={"sec": sec_down}, device_id_type=MESH)

    load_u.wait()

    def remote(src, dst, send, recv, target):
        return pltpu.make_async_remote_copy(
            src_ref=src, dst_ref=dst, send_sem=send, recv_sem=recv,
            device_id=target, device_id_type=MESH,
        )

    lane = lax.broadcasted_iota(jnp.int32, (16, 128), 1)
    row = lax.broadcasted_iota(jnp.int32, (8, 256), 0)

    def fresh(tick, f):
        halves = [f_recv[tick, h, f].astype(jnp.float32) for h in range(2)]
        return pltpu.roll(jnp.concatenate(halves, axis=1), 64, 1)

    copies = []
    for tick in range(TICKS):
        now = u.at[tick]
        for f in range(5):
            first, last = now[f, :, 0:128], now[f, :, 128:256]
            y_send[tick, 0, f] = jnp.where(
                lane < 64, first[0:16], pltpu.roll(first[16:32], 64, 1)
            ).astype(jnp.bfloat16)
            y_send[tick, 1, f] = jnp.where(
                lane < 64, pltpu.roll(last[16:32], 64, 1), last[0:16]
            ).astype(jnp.bfloat16)
        if tick == 0:
            pl.semaphore_wait(
                barrier, 4 + has_up.astype(jnp.int32) + has_down.astype(jnp.int32)
            )
        to_y = (
            remote(y_send.at[tick, 0], y_hi.at[tick], y_ss.at[tick, 0], y_rs.at[tick, 0], {"gy": gy_down}),
            remote(y_send.at[tick, 1], y_lo.at[tick], y_ss.at[tick, 1], y_rs.at[tick, 1], {"gy": gy_up}),
        )
        to_x = (
            remote(now.at[:, 0:8], x_hi.at[tick], x_ss.at[tick, 0], x_rs.at[tick, 0], {"gx": gx_down}),
            remote(now.at[:, 24:32], x_lo.at[tick], x_ss.at[tick, 1], x_rs.at[tick, 1], {"gx": gx_up}),
        )
        for copy in to_y + to_x:
            copy.start()
        copies += to_y + to_x

        for half in range(2):
            cols = slice(128 * half, 128 * half + 128)
            prims = primitives(*(now[f, :, cols] for f in range(5)))
            for f, term in enumerate(flux_difference(2, prims, z_difference)):
                rate[f, :, cols] = term

        main = primitives(*(now[f] for f in range(5)))
        inner = flux_difference(1, main, ring_difference(1, NZ))
        for f in range(5):
            inside[f] = pltpu.roll(inner[f], 192, 1)[:, 0:128]
        for copy in to_x:
            copy.wait_recv()
        halo = primitives(
            *(jnp.where(row < 4, x_hi[tick, f], x_lo[tick, f]) for f in range(5))
        )
        ring = tree_concat(main, halo, 0)
        for f, term in enumerate(flux_difference(0, ring, ring_difference(0, 1))):
            part = rate[f] + term[0:32]
            rate[f] = part
            whole = pltpu.roll(part, 192, 1)[:, 0:128] + inside[f]
            inside[f] = whole
            f_send[tick, 0, f] = whole.astype(jnp.bfloat16)

        to_next = [
            remote(
                f_send.at[tick, h], f_recv.at[tick, h], f_ss.at[tick, h], f_rs.at[tick, h],
                {"sec": sec_up},
            )
            for h in range(2)
        ]

        @pl.when(has_up)
        def _():
            to_next[0].start()

        for copy in to_y:
            copy.wait_recv()
        sides = []
        for f in range(5):
            high = y_hi[tick, f].astype(jnp.float32)
            low = y_lo[tick, f].astype(jnp.float32)
            top = jnp.where(lane < 64, high, low)
            bottom = pltpu.roll(jnp.where(lane < 64, low, high), 64, 1)
            sides.append(jnp.concatenate([top, bottom], axis=0))
        ring = tree_concat(main, primitives(*sides), 1)
        terms = flux_difference(1, ring, ring_difference(1, NZ))
        for f, term in enumerate(terms):
            own = rate[f] + term[:, 0:256]
            rate[f] = own
            f_send[tick, 1, f] = pltpu.roll(own, 64, 1)[:, 0:128].astype(jnp.bfloat16)

        @pl.when(has_up)
        def _():
            to_next[1].start()

        if tick == 0:
            load_st.wait()
        target = out.at[0] if tick == TICKS - 1 else u.at[tick + 1]

        @pl.when(level == 0)
        def _():
            for f in range(5):
                target[f] = now[f] + TIME_STEP * rate[f]

        @pl.when(has_down)
        def _():
            def past(h, f):
                return st[h, f].astype(jnp.float32) if h < 3 else fresh(h - 3, f)

            for f in range(5):
                known = W0 * past(tick, f) + W1 * past(tick + 1, f) + W2 * past(tick + 2, f)
                rate[f] = now[f] + TIME_STEP * (rate[f] + known)
            for copy in to_next:
                copy.wait_recv()
            for f in range(5):
                target[f] = rate[f] + (TIME_STEP * W3) * fresh(tick, f)

        @pl.when(has_up)
        def _():
            for copy in to_next:
                copy.wait_send()

    for copy in copies:
        copy.wait_send()


def solution(mesh):
    counts = tuple(mesh.shape[name] for name in ("sec", "gx", "gy"))

    def per_device(fields, stored_rates):
        _, _, rows, cols = fields.shape
        halo_x = pltpu.VMEM((TICKS, 5, 8, cols), jnp.float32)
        halo_y = pltpu.VMEM((TICKS, 5, rows // 2, 128), jnp.bfloat16)
        block = (5, rows, cols)
        level_half = pltpu.VMEM((TICKS, 2, 5, rows, 128), jnp.bfloat16)
        return pl.pallas_call(
            lambda *refs: kernel(counts, *refs),
            name="correct",
            out_shape=jax.ShapeDtypeStruct(fields.shape, fields.dtype),
            in_specs=[pl.BlockSpec(memory_space=pl.ANY)] * 2,
            out_specs=pl.BlockSpec(memory_space=pltpu.VMEM),
            scratch_shapes=[
                pltpu.VMEM((TICKS,) + block, jnp.float32),
                pltpu.VMEM((3,) + block, jnp.bfloat16),
                pltpu.VMEM(block, jnp.float32),
                pltpu.VMEM((5, rows, 128), jnp.float32),
                halo_x,
                halo_x,
                pltpu.VMEM((TICKS, 2, 5, rows // 2, 128), jnp.bfloat16),
                halo_y,
                halo_y,
                level_half,
                level_half,
                pltpu.SemaphoreType.DMA((2,)),
                pltpu.SemaphoreType.DMA((TICKS, 2)),
                pltpu.SemaphoreType.DMA((TICKS, 2)),
                pltpu.SemaphoreType.DMA((TICKS, 2)),
                pltpu.SemaphoreType.DMA((TICKS, 2)),
                pltpu.SemaphoreType.DMA((TICKS, 2)),
                pltpu.SemaphoreType.DMA((TICKS, 2)),
            ],
            compiler_params=pltpu.CompilerParams(collective_id=0, has_side_effects=True),
        )(fields, stored_rates)

    return jax.shard_map(
        per_device,
        mesh=mesh,
        in_specs=(P("sec", None, "gx", "gy"), P("sec", None, None, "gx", "gy")),
        out_specs=P("sec", None, "gx", "gy"),
        check_vma=False,
    )
```

```python
import jax
import jax.numpy as jnp
from jax import lax
from jax.experimental import pallas as pl
from jax.experimental.pallas import tpu as pltpu
from jax.sharding import PartitionSpec as P

NZ = 32
TICKS = 3
LEVELS = 4
TIME_STEP = 0.04
DYNAMIC_FRICTION = 0.4
CONDUCTIVITY = 0.5
GAMMA_LESS = 0.4
W0, W1, W2, W3 = 1.0 / 24.0, -5.0 / 24.0, 19.0 / 24.0 - 1.0, 9.0 / 24.0
MESH = pl.DeviceIdType.MESH


def primitives(density, mom_x, mom_y, mom_z, energy):
    inverse = 1.0 / density
    vel = (mom_x * inverse, mom_y * inverse, mom_z * inverse)
    kinetic = 0.5 * (vel[0] * vel[0] + vel[1] * vel[1] + vel[2] * vel[2])
    pressure = GAMMA_LESS * (energy - density * kinetic)
    heat = DYNAMIC_FRICTION * kinetic + CONDUCTIVITY * (pressure * inverse)
    return (mom_x, mom_y, mom_z), vel, pressure, energy + pressure, heat


def flux_difference(axis, prims, difference):
    mom, vel, pressure, enthalpy, heat = prims
    terms = [difference(mom[axis]) * -0.5]
    for c in range(3):
        flux = mom[c] * vel[axis]
        if c == axis:
            flux = flux + pressure
        spread = difference(vel[c]) * (0.5 * DYNAMIC_FRICTION)
        terms.append(difference(spread - flux) * 0.5)
    spread = difference(heat) * 0.5
    terms.append(difference(spread - enthalpy * vel[axis]) * 0.5)
    return terms


def ring_difference(axis, step):
    def difference(values):
        size = values.shape[axis]
        return pltpu.roll(values, size - step, axis) - pltpu.roll(values, step, axis)

    return difference


def z_difference(values):
    lane = lax.broadcasted_iota(jnp.int32, values.shape, 1) % NZ
    up = jnp.where(
        lane < NZ - 1, pltpu.roll(values, 127, 1), pltpu.roll(values, NZ - 1, 1)
    )
    down = jnp.where(lane > 0, pltpu.roll(values, 1, 1), pltpu.roll(values, 129 - NZ, 1))
    return up - down


def halo_terms(axis, prims, cell, array_axis, step):
    mom, vel, pressure, enthalpy, heat = prims
    size = cell.shape[array_axis]

    def outer(flux):
        after = pltpu.roll(flux, step, array_axis)
        before = pltpu.roll(flux, size - step, array_axis)
        return jnp.where(cell == 1, -0.5 * after, jnp.where(cell == 6, 0.5 * before, 0.0))

    terms = [outer(mom[axis])]
    for c in range(3):
        flux = mom[c] * vel[axis]
        if c == axis:
            flux = flux + pressure
        terms.append(outer(flux) + (0.25 * DYNAMIC_FRICTION) * vel[c])
    terms.append(outer(enthalpy * vel[axis]) + 0.25 * heat)
    return terms


def kernel(
    counts, fields, stored, out, u, st, rate, x_lo, x_hi, y_send, y_lo, y_hi,
    f_send, f_recv, load_sem, x_ss, x_rs, y_ss, y_rs, f_ss, f_rs,
):
    n_sec, n_gx, n_gy = counts
    sec, gx, gy = lax.axis_index("sec"), lax.axis_index("gx"), lax.axis_index("gy")
    level = lax.rem(sec, LEVELS)
    gx_up, gx_down = lax.rem(gx + 1, n_gx), lax.rem(gx + n_gx - 1, n_gx)
    gy_up, gy_down = lax.rem(gy + 1, n_gy), lax.rem(gy + n_gy - 1, n_gy)
    sec_up, sec_down = lax.rem(sec + 1, n_sec), lax.rem(sec + n_sec - 1, n_sec)
    has_up, has_down = level < LEVELS - 1, level > 0

    load_u = pltpu.make_async_copy(fields.at[0], u.at[0], load_sem.at[0])
    load_st = pltpu.make_async_copy(stored.at[0], st, load_sem.at[1])
    load_u.start()
    load_st.start()

    barrier = pltpu.get_barrier_semaphore()
    for target in ({"gx": gx_up}, {"gx": gx_down}, {"gy": gy_up}, {"gy": gy_down}):
        pl.semaphore_signal(barrier, inc=1, device_id=target, device_id_type=MESH)

    @pl.when(has_up)
    def _():
        pl.semaphore_signal(barrier, inc=1, device_id={"sec": sec_up}, device_id_type=MESH)

    @pl.when(has_down)
    def _():
        pl.semaphore_signal(barrier, inc=1, device_id={"sec": sec_down}, device_id_type=MESH)

    load_u.wait()

    def remote(src, dst, send, recv, target):
        return pltpu.make_async_remote_copy(
            src_ref=src, dst_ref=dst, send_sem=send, recv_sem=recv,
            device_id=target, device_id_type=MESH,
        )

    lane = lax.broadcasted_iota(jnp.int32, (16, 128), 1)
    row = lax.broadcasted_iota(jnp.int32, (8, 256), 0)
    lane_all = lax.broadcasted_iota(jnp.int32, (32, 128), 1)
    side = lane_all // NZ
    side = jnp.where(side < 2, side, side + 4)

    def fresh(tick, f):
        halves = [f_recv[tick, h, f].astype(jnp.float32) for h in range(2)]
        return pltpu.roll(jnp.concatenate(halves, axis=1), 64, 1)

    copies = []
    for tick in range(TICKS):
        now = u.at[tick]
        for f in range(5):
            first, last = now[f, :, 0:128], now[f, :, 128:256]
            y_send[tick, 0, f] = jnp.where(
                lane < 64, first[0:16], pltpu.roll(first[16:32], 64, 1)
            ).astype(jnp.bfloat16)
            y_send[tick, 1, f] = jnp.where(
                lane < 64, pltpu.roll(last[16:32], 64, 1), last[0:16]
            ).astype(jnp.bfloat16)
        if tick == 0:
            pl.semaphore_wait(
                barrier, 4 + has_up.astype(jnp.int32) + has_down.astype(jnp.int32)
            )
        to_y = (
            remote(y_send.at[tick, 0], y_hi.at[tick], y_ss.at[tick, 0], y_rs.at[tick, 0], {"gy": gy_down}),
            remote(y_send.at[tick, 1], y_lo.at[tick], y_ss.at[tick, 1], y_rs.at[tick, 1], {"gy": gy_up}),
        )
        to_x = (
            remote(now.at[:, 0:8], x_hi.at[tick], x_ss.at[tick, 0], x_rs.at[tick, 0], {"gx": gx_down}),
            remote(now.at[:, 24:32], x_lo.at[tick], x_ss.at[tick, 1], x_rs.at[tick, 1], {"gx": gx_up}),
        )
        for copy in to_y + to_x:
            copy.start()
        copies += to_y + to_x

        for half in range(2):
            cols = slice(128 * half, 128 * half + 128)
            prims = primitives(*(now[f, :, cols] for f in range(5)))
            for f, term in enumerate(flux_difference(2, prims, z_difference)):
                rate[f, :, cols] = term
        main = primitives(*(now[f] for f in range(5)))
        for axis, array_axis, step in ((0, 0, 1), (1, 1, NZ)):
            zeros = jnp.zeros((8, 256) if axis == 0 else (32, 128), jnp.float32)
            ring = jax.tree.map(
                lambda v: jnp.concatenate([v, zeros], axis=array_axis), main
            )
            terms = flux_difference(axis, ring, ring_difference(array_axis, step))
            for f in range(5):
                rate[f] += terms[f][0:32, 0:256]

        for copy in to_x:
            copy.wait_recv()
        prims = primitives(
            *(jnp.where(row < 4, x_hi[tick, f], x_lo[tick, f]) for f in range(5))
        )
        for f, term in enumerate(halo_terms(0, prims, row, 0, 1)):
            rate[f, 0:8] += jnp.where(row < 2, pltpu.roll(term, 2, 0), 0.0)
            rate[f, 24:32] += jnp.where(row >= 6, pltpu.roll(term, 6, 0), 0.0)
        for f in range(5):
            f_send[tick, 0, f] = pltpu.roll(rate[f], 192, 1)[:, 0:128].astype(jnp.bfloat16)

        to_next = [
            remote(
                f_send.at[tick, h], f_recv.at[tick, h], f_ss.at[tick, h], f_rs.at[tick, h],
                {"sec": sec_up},
            )
            for h in range(2)
        ]

        @pl.when(has_up)
        def _():
            to_next[0].start()

        for copy in to_y:
            copy.wait_recv()
        sides = []
        for f in range(5):
            high = y_hi[tick, f].astype(jnp.float32)
            low = y_lo[tick, f].astype(jnp.float32)
            top = jnp.where(lane < 64, high, low)
            bottom = pltpu.roll(jnp.where(lane < 64, low, high), 64, 1)
            sides.append(jnp.concatenate([top, bottom], axis=0))
        edges = halo_terms(1, primitives(*sides), side, 1, NZ)
        for f in range(5):
            own = pltpu.roll(rate[f], 64, 1)[:, 0:128] + edges[f]
            f_send[tick, 1, f] = own.astype(jnp.bfloat16)

        @pl.when(has_up)
        def _():
            to_next[1].start()

        for f in range(5):
            edge = pltpu.roll(edges[f], 64, 1)
            rate[f, :, 0:128] += jnp.where(lane_all < 64, edge, 0.0)
            rate[f, :, 128:256] += jnp.where(lane_all >= 64, edge, 0.0)

        if tick == 0:
            load_st.wait()
        target = out.at[0] if tick == TICKS - 1 else u.at[tick + 1]

        @pl.when(level == 0)
        def _():
            for f in range(5):
                target[f] = now[f] + TIME_STEP * rate[f]

        @pl.when(has_down)
        def _():
            def past(h, f):
                return st[h, f].astype(jnp.float32) if h < 3 else fresh(h - 3, f)

            for f in range(5):
                known = W0 * past(tick, f) + W1 * past(tick + 1, f) + W2 * past(tick + 2, f)
                rate[f] = now[f] + TIME_STEP * (rate[f] + known)
            for copy in to_next:
                copy.wait_recv()
            for f in range(5):
                target[f] = rate[f] + (TIME_STEP * W3) * fresh(tick, f)

        @pl.when(has_up)
        def _():
            for copy in to_next:
                copy.wait_send()

    for copy in copies:
        copy.wait_send()


def solution(mesh):
    counts = tuple(mesh.shape[name] for name in ("sec", "gx", "gy"))

    def per_device(fields, stored_rates):
        _, _, rows, cols = fields.shape
        halo_x = pltpu.VMEM((TICKS, 5, 8, cols), jnp.float32)
        halo_y = pltpu.VMEM((TICKS, 5, rows // 2, 128), jnp.bfloat16)
        block = (5, rows, cols)
        level_half = pltpu.VMEM((TICKS, 2, 5, rows, 128), jnp.bfloat16)
        return pl.pallas_call(
            lambda *refs: kernel(counts, *refs),
            name="correct",
            out_shape=pltpu.VMEM(fields.shape, fields.dtype),
            in_specs=[pl.BlockSpec(memory_space=pl.ANY)] * 2,
            out_specs=pl.BlockSpec(memory_space=pltpu.VMEM),
            scratch_shapes=[
                pltpu.VMEM((TICKS,) + block, jnp.float32),
                pltpu.VMEM((3,) + block, jnp.bfloat16),
                pltpu.VMEM(block, jnp.float32),
                halo_x,
                halo_x,
                pltpu.VMEM((TICKS, 2, 5, rows // 2, 128), jnp.bfloat16),
                halo_y,
                halo_y,
                level_half,
                level_half,
                pltpu.SemaphoreType.DMA((2,)),
                pltpu.SemaphoreType.DMA((TICKS, 2)),
                pltpu.SemaphoreType.DMA((TICKS, 2)),
                pltpu.SemaphoreType.DMA((TICKS, 2)),
                pltpu.SemaphoreType.DMA((TICKS, 2)),
                pltpu.SemaphoreType.DMA((TICKS, 2)),
                pltpu.SemaphoreType.DMA((TICKS, 2)),
            ],
            compiler_params=pltpu.CompilerParams(collective_id=0, has_side_effects=True),
        )(fields, stored_rates)

    return jax.shard_map(
        per_device,
        mesh=mesh,
        in_specs=(P("sec", None, "gx", "gy"), P("sec", None, None, "gx", "gy")),
        out_specs=P("sec", None, "gx", "gy"),
        check_vma=False,
    )
```

```python
import jax
import jax.numpy as jnp
from jax import lax
from jax.experimental import pallas as pl
from jax.experimental.pallas import tpu as pltpu
from jax.sharding import PartitionSpec as P

NZ = 32
TICKS = 3
LEVELS = 4
TIME_STEP = 0.04
DYNAMIC_FRICTION = 0.4
CONDUCTIVITY = 0.5
GAMMA_LESS = 0.4
W0, W1, W2, W3 = 1.0 / 24.0, -5.0 / 24.0, 19.0 / 24.0 - 1.0, 9.0 / 24.0
MESH = pl.DeviceIdType.MESH


def primitives(density, mom_x, mom_y, mom_z, energy):
    inverse = 1.0 / density
    vel = (mom_x * inverse, mom_y * inverse, mom_z * inverse)
    kinetic = 0.5 * (vel[0] * vel[0] + vel[1] * vel[1] + vel[2] * vel[2])
    pressure = GAMMA_LESS * (energy - density * kinetic)
    heat = DYNAMIC_FRICTION * kinetic + CONDUCTIVITY * (pressure * inverse)
    return (mom_x, mom_y, mom_z), vel, pressure, energy + pressure, heat


def flux_difference(axis, prims, difference):
    mom, vel, pressure, enthalpy, heat = prims
    terms = [difference(mom[axis]) * -0.5]
    for c in range(3):
        flux = mom[c] * vel[axis]
        if c == axis:
            flux = flux + pressure
        spread = difference(vel[c]) * (0.5 * DYNAMIC_FRICTION)
        terms.append(difference(spread - flux) * 0.5)
    spread = difference(heat) * 0.5
    terms.append(difference(spread - enthalpy * vel[axis]) * 0.5)
    return terms


def ring_difference(axis, step):
    def difference(values):
        size = values.shape[axis]
        return pltpu.roll(values, size - step, axis) - pltpu.roll(values, step, axis)

    return difference


def z_difference(values):
    lane = lax.broadcasted_iota(jnp.int32, values.shape, 1) % NZ
    up = jnp.where(
        lane < NZ - 1, pltpu.roll(values, 127, 1), pltpu.roll(values, NZ - 1, 1)
    )
    down = jnp.where(lane > 0, pltpu.roll(values, 1, 1), pltpu.roll(values, 129 - NZ, 1))
    return up - down


def halo_terms(axis, prims, cell, array_axis, step):
    mom, vel, pressure, enthalpy, heat = prims
    size = cell.shape[array_axis]

    def outer(flux):
        after = pltpu.roll(flux, step, array_axis)
        before = pltpu.roll(flux, size - step, array_axis)
        return jnp.where(cell == 1, -0.5 * after, jnp.where(cell == 6, 0.5 * before, 0.0))

    terms = [outer(mom[axis])]
    for c in range(3):
        flux = mom[c] * vel[axis]
        if c == axis:
            flux = flux + pressure
        terms.append(outer(flux) + (0.25 * DYNAMIC_FRICTION) * vel[c])
    terms.append(outer(enthalpy * vel[axis]) + 0.25 * heat)
    return terms


def kernel(
    counts, fields, stored, out, u, st, rate, x_lo, x_hi, y_send, y_lo, y_hi,
    f_send, f_recv, c_send, c_recv, d_lo, d_hi, past_fresh,
    load_sem, x_ss, x_rs, y_ss, y_rs, f_ss, f_rs, c_ss, c_rs, d_ss, d_rs,
):
    n_sec, n_gx, n_gy = counts
    sec, gx, gy = lax.axis_index("sec"), lax.axis_index("gx"), lax.axis_index("gy")
    level = lax.rem(sec, LEVELS)
    gx_up, gx_down = lax.rem(gx + 1, n_gx), lax.rem(gx + n_gx - 1, n_gx)
    gy_up, gy_down = lax.rem(gy + 1, n_gy), lax.rem(gy + n_gy - 1, n_gy)
    sec_up, sec_down = lax.rem(sec + 1, n_sec), lax.rem(sec + n_sec - 1, n_sec)
    has_up, has_down = level < LEVELS - 1, level > 0

    load_u = pltpu.make_async_copy(fields.at[0], u.at[0], load_sem.at[0])
    load_st = pltpu.make_async_copy(stored.at[0], st, load_sem.at[1])
    load_u.start()
    load_st.start()

    barrier = pltpu.get_barrier_semaphore()
    for target in ({"gx": gx_up}, {"gx": gx_down}, {"gy": gy_up}, {"gy": gy_down}):
        pl.semaphore_signal(barrier, inc=1, device_id=target, device_id_type=MESH)

    @pl.when(has_up)
    def _():
        for target in ({"sec": sec_up}, {"sec": sec_up, "gy": gy_up}, {"sec": sec_up, "gy": gy_down}):
            pl.semaphore_signal(barrier, inc=1, device_id=target, device_id_type=MESH)

    @pl.when(has_down)
    def _():
        for target in ({"sec": sec_down}, {"sec": sec_down, "gy": gy_up}, {"sec": sec_down, "gy": gy_down}):
            pl.semaphore_signal(barrier, inc=1, device_id=target, device_id_type=MESH)

    load_u.wait()

    def remote(src, dst, send, recv, target):
        return pltpu.make_async_remote_copy(
            src_ref=src, dst_ref=dst, send_sem=send, recv_sem=recv,
            device_id=target, device_id_type=MESH,
        )

    lane = lax.broadcasted_iota(jnp.int32, (16, 128), 1)
    row = lax.broadcasted_iota(jnp.int32, (8, 256), 0)
    lane_all = lax.broadcasted_iota(jnp.int32, (32, 128), 1)
    side = lane_all // NZ
    side = jnp.where(side < 2, side, side + 4)

    def y_edges(low, high):
        sides = []
        for f in range(5):
            above, below = high[f].astype(jnp.float32), low[f].astype(jnp.float32)
            top = jnp.where(lane < 64, above, below)
            bottom = pltpu.roll(jnp.where(lane < 64, below, above), 64, 1)
            sides.append(jnp.concatenate([top, bottom], axis=0))
        return halo_terms(1, primitives(*sides), side, 1, NZ)

    def add_y(to, edges):
        for f in range(5):
            edge = pltpu.roll(edges[f], 64, 1)
            to[f, :, 0:128] += jnp.where(lane_all < 64, edge, 0.0)
            to[f, :, 128:256] += jnp.where(lane_all >= 64, edge, 0.0)

    def add_x(to, f, term):
        to[f, 0:8] += jnp.where(row < 2, pltpu.roll(term, 2, 0), 0.0)
        to[f, 24:32] += jnp.where(row >= 6, pltpu.roll(term, 6, 0), 0.0)

    copies, up_copies = [], ()
    for tick in range(TICKS):
        now = u.at[tick]
        for f in range(5):
            first, last = now[f, :, 0:128], now[f, :, 128:256]
            y_send[tick, 0, f] = jnp.where(
                lane < 64, first[0:16], pltpu.roll(first[16:32], 64, 1)
            ).astype(jnp.bfloat16)
            y_send[tick, 1, f] = jnp.where(
                lane < 64, pltpu.roll(last[16:32], 64, 1), last[0:16]
            ).astype(jnp.bfloat16)
        if tick == 0:
            pl.semaphore_wait(
                barrier, 4 + 3 * has_up.astype(jnp.int32) + 3 * has_down.astype(jnp.int32)
            )
        to_y = (
            remote(y_send.at[tick, 0], y_hi.at[tick], y_ss.at[tick, 0], y_rs.at[tick, 0], {"gy": gy_down}),
            remote(y_send.at[tick, 1], y_lo.at[tick], y_ss.at[tick, 1], y_rs.at[tick, 1], {"gy": gy_up}),
        )
        to_x = (
            remote(now.at[:, 0:8], x_hi.at[tick], x_ss.at[tick, 0], x_rs.at[tick, 0], {"gx": gx_down}),
            remote(now.at[:, 24:32], x_lo.at[tick], x_ss.at[tick, 1], x_rs.at[tick, 1], {"gx": gx_up}),
        )
        diagonal = (
            remote(y_send.at[tick, 0], d_hi.at[tick], d_ss.at[tick, 0], d_rs.at[tick, 0], {"sec": sec_up, "gy": gy_down}),
            remote(y_send.at[tick, 1], d_lo.at[tick], d_ss.at[tick, 1], d_rs.at[tick, 1], {"sec": sec_up, "gy": gy_up}),
        )
        to_next = remote(
            f_send.at[tick], f_recv.at[tick], f_ss.at[tick], f_rs.at[tick], {"sec": sec_up}
        )
        x_next = remote(
            c_send.at[tick], c_recv.at[tick], c_ss.at[tick], c_rs.at[tick], {"sec": sec_up}
        )
        for copy in to_y + to_x:
            copy.start()

        @pl.when(has_up)
        def _():
            for copy in diagonal:
                copy.start()

        copies += to_y + to_x
        up_copies += (to_next, x_next) + diagonal

        for half in range(2):
            cols = slice(128 * half, 128 * half + 128)
            prims = primitives(*(now[f, :, cols] for f in range(5)))
            for f, term in enumerate(flux_difference(2, prims, z_difference)):
                rate[f, :, cols] = term
        main = primitives(*(now[f] for f in range(5)))
        for axis, array_axis, step in ((0, 0, 1), (1, 1, NZ)):
            zeros = jnp.zeros((8, 256) if axis == 0 else (32, 128), jnp.float32)
            ring = jax.tree.map(
                lambda v: jnp.concatenate([v, zeros], axis=array_axis), main
            )
            terms = flux_difference(axis, ring, ring_difference(array_axis, step))
            for f in range(5):
                total = rate[f] + terms[f][0:32, 0:256]
                rate[f] = total
                if axis == 1:
                    f_send[tick, f] = total.astype(jnp.bfloat16)

        @pl.when(has_up)
        def _():
            to_next.start()

        for copy in to_x:
            copy.wait_recv()
        prims = primitives(
            *(jnp.where(row < 4, x_hi[tick, f], x_lo[tick, f]) for f in range(5))
        )
        for f, term in enumerate(halo_terms(0, prims, row, 0, 1)):
            c_send[tick, f] = term.astype(jnp.bfloat16)
            add_x(rate, f, term)

        @pl.when(has_up)
        def _():
            x_next.start()

        for copy in to_y:
            copy.wait_recv()
        add_y(rate, y_edges(y_lo[tick], y_hi[tick]))

        if tick == 0:
            load_st.wait()
        target = out.at[0] if tick == TICKS - 1 else u.at[tick + 1]

        @pl.when(level == 0)
        def _():
            for f in range(5):
                target[f] = now[f] + TIME_STEP * rate[f]

        @pl.when(has_down)
        def _():
            def past(h, f):
                return st[h, f].astype(jnp.float32) if h < 3 else past_fresh[h - 3, f]

            for f in range(5):
                known = W0 * past(tick, f) + W1 * past(tick + 1, f) + W2 * past(tick + 2, f)
                rate[f] = now[f] + TIME_STEP * (rate[f] + known)
            new = past_fresh.at[tick]
            to_next.wait_recv()
            for f in range(5):
                new[f] = f_recv[tick, f].astype(jnp.float32)
            x_next.wait_recv()
            for f in range(5):
                add_x(new, f, c_recv[tick, f].astype(jnp.float32))
            for copy in diagonal:
                copy.wait_recv()
            add_y(new, y_edges(d_lo[tick], d_hi[tick]))
            for f in range(5):
                target[f] = rate[f] + (TIME_STEP * W3) * new[f]

    @pl.when(has_up)
    def _():
        for copy in up_copies:
            copy.wait_send()

    for copy in copies:
        copy.wait_send()


def solution(mesh):
    counts = tuple(mesh.shape[name] for name in ("sec", "gx", "gy"))

    def per_device(fields, stored_rates):
        _, _, rows, cols = fields.shape
        halo_x = pltpu.VMEM((TICKS, 5, 8, cols), jnp.float32)
        halo_y = pltpu.VMEM((TICKS, 5, rows // 2, 128), jnp.bfloat16)
        block = (5, rows, cols)
        level_block = pltpu.VMEM((TICKS,) + block, jnp.bfloat16)
        x_terms = pltpu.VMEM((TICKS, 5, 8, cols), jnp.bfloat16)
        return pl.pallas_call(
            lambda *refs: kernel(counts, *refs),
            name="correct",
            out_shape=pltpu.VMEM(fields.shape, fields.dtype),
            in_specs=[pl.BlockSpec(memory_space=pl.ANY)] * 2,
            out_specs=pl.BlockSpec(memory_space=pltpu.VMEM),
            scratch_shapes=[
                pltpu.VMEM((TICKS,) + block, jnp.float32),
                pltpu.VMEM((3,) + block, jnp.bfloat16),
                pltpu.VMEM(block, jnp.float32),
                halo_x,
                halo_x,
                pltpu.VMEM((TICKS, 2, 5, rows // 2, 128), jnp.bfloat16),
                halo_y,
                halo_y,
                level_block,
                level_block,
                x_terms,
                x_terms,
                halo_y,
                halo_y,
                pltpu.VMEM((TICKS,) + block, jnp.float32),
                pltpu.SemaphoreType.DMA((2,)),
                pltpu.SemaphoreType.DMA((TICKS, 2)),
                pltpu.SemaphoreType.DMA((TICKS, 2)),
                pltpu.SemaphoreType.DMA((TICKS, 2)),
                pltpu.SemaphoreType.DMA((TICKS, 2)),
                pltpu.SemaphoreType.DMA((TICKS,)),
                pltpu.SemaphoreType.DMA((TICKS,)),
                pltpu.SemaphoreType.DMA((TICKS,)),
                pltpu.SemaphoreType.DMA((TICKS,)),
                pltpu.SemaphoreType.DMA((TICKS, 2)),
                pltpu.SemaphoreType.DMA((TICKS, 2)),
            ],
            compiler_params=pltpu.CompilerParams(collective_id=0, has_side_effects=True),
        )(fields, stored_rates)

    return jax.shard_map(
        per_device,
        mesh=mesh,
        in_specs=(P("sec", None, "gx", "gy"), P("sec", None, None, "gx", "gy")),
        out_specs=P("sec", None, "gx", "gy"),
        check_vma=False,
    )
```

```python
import jax
import jax.numpy as jnp
from jax import lax
from jax.experimental import pallas as pl
from jax.experimental.pallas import tpu as pltpu
from jax.sharding import PartitionSpec as P

NZ = 32
TICKS = 3
LEVELS = 4
TIME_STEP = 0.04
DYNAMIC_FRICTION = 0.4
CONDUCTIVITY = 0.5
GAMMA_LESS = 0.4
W0, W1, W2, W3 = 1.0 / 24.0, -5.0 / 24.0, 19.0 / 24.0 - 1.0, 9.0 / 24.0
MESH = pl.DeviceIdType.MESH


def primitives(density, mom_x, mom_y, mom_z, energy):
    inverse = 1.0 / density
    vel = (mom_x * inverse, mom_y * inverse, mom_z * inverse)
    kinetic = 0.5 * (vel[0] * vel[0] + vel[1] * vel[1] + vel[2] * vel[2])
    pressure = GAMMA_LESS * (energy - density * kinetic)
    heat = DYNAMIC_FRICTION * kinetic + CONDUCTIVITY * (pressure * inverse)
    return (mom_x, mom_y, mom_z), vel, pressure, energy + pressure, heat


def flux_difference(axis, prims, difference):
    mom, vel, pressure, enthalpy, heat = prims
    terms = [difference(mom[axis]) * -0.5]
    for c in range(3):
        flux = mom[c] * vel[axis]
        if c == axis:
            flux = flux + pressure
        spread = difference(vel[c]) * (0.5 * DYNAMIC_FRICTION)
        terms.append(difference(spread - flux) * 0.5)
    spread = difference(heat) * 0.5
    terms.append(difference(spread - enthalpy * vel[axis]) * 0.5)
    return terms


def ring_difference(axis, step):
    def difference(values):
        size = values.shape[axis]
        return pltpu.roll(values, size - step, axis) - pltpu.roll(values, step, axis)

    return difference


def z_difference(values):
    lane = lax.broadcasted_iota(jnp.int32, values.shape, 1) % NZ
    up = jnp.where(
        lane < NZ - 1, pltpu.roll(values, 127, 1), pltpu.roll(values, NZ - 1, 1)
    )
    down = jnp.where(lane > 0, pltpu.roll(values, 1, 1), pltpu.roll(values, 129 - NZ, 1))
    return up - down


def halo_terms(axis, prims, cell, array_axis, step):
    mom, vel, pressure, enthalpy, heat = prims
    size = cell.shape[array_axis]

    def outer(flux):
        after = pltpu.roll(flux, step, array_axis)
        before = pltpu.roll(flux, size - step, array_axis)
        return jnp.where(cell == 1, -0.5 * after, jnp.where(cell == 6, 0.5 * before, 0.0))

    terms = [outer(mom[axis])]
    for c in range(3):
        flux = mom[c] * vel[axis]
        if c == axis:
            flux = flux + pressure
        terms.append(outer(flux) + (0.25 * DYNAMIC_FRICTION) * vel[c])
    terms.append(outer(enthalpy * vel[axis]) + 0.25 * heat)
    return terms


def kernel(
    counts, fields, stored, out, u, st, rate, x_lo, x_hi, y_send, y_lo, y_hi,
    f_send, f_recv, c_send, c_recv, d_lo, d_hi, past_fresh,
    load_sem, x_ss, x_rs, y_ss, y_rs, f_ss, f_rs, c_ss, c_rs, d_ss, d_rs,
):
    n_sec, n_gx, n_gy = counts
    sec, gx, gy = lax.axis_index("sec"), lax.axis_index("gx"), lax.axis_index("gy")
    level = lax.rem(sec, LEVELS)
    gx_up, gx_down = lax.rem(gx + 1, n_gx), lax.rem(gx + n_gx - 1, n_gx)
    gy_up, gy_down = lax.rem(gy + 1, n_gy), lax.rem(gy + n_gy - 1, n_gy)
    sec_up, sec_down = lax.rem(sec + 1, n_sec), lax.rem(sec + n_sec - 1, n_sec)
    has_up, has_down = level < LEVELS - 1, level > 0

    load_u = pltpu.make_async_copy(fields.at[0], u.at[0], load_sem.at[0])
    load_st = pltpu.make_async_copy(stored.at[0], st, load_sem.at[1])
    load_u.start()
    load_st.start()

    barrier = pltpu.get_barrier_semaphore()
    for target in ({"gx": gx_up}, {"gx": gx_down}, {"gy": gy_up}, {"gy": gy_down}):
        pl.semaphore_signal(barrier, inc=1, device_id=target, device_id_type=MESH)

    @pl.when(has_up)
    def _():
        for target in ({"sec": sec_up}, {"sec": sec_up, "gy": gy_up}, {"sec": sec_up, "gy": gy_down}):
            pl.semaphore_signal(barrier, inc=1, device_id=target, device_id_type=MESH)

    @pl.when(has_down)
    def _():
        for target in ({"sec": sec_down}, {"sec": sec_down, "gy": gy_up}, {"sec": sec_down, "gy": gy_down}):
            pl.semaphore_signal(barrier, inc=1, device_id=target, device_id_type=MESH)

    load_u.wait()

    def remote(src, dst, send, recv, target):
        return pltpu.make_async_remote_copy(
            src_ref=src, dst_ref=dst, send_sem=send, recv_sem=recv,
            device_id=target, device_id_type=MESH,
        )

    lane = lax.broadcasted_iota(jnp.int32, (16, 128), 1)
    row = lax.broadcasted_iota(jnp.int32, (8, 256), 0)
    lane_all = lax.broadcasted_iota(jnp.int32, (32, 128), 1)
    side = lane_all // NZ
    side = jnp.where(side < 2, side, side + 4)

    def y_edges(low, high):
        sides = []
        for f in range(5):
            above, below = high[f].astype(jnp.float32), low[f].astype(jnp.float32)
            top = jnp.where(lane < 64, above, below)
            bottom = pltpu.roll(jnp.where(lane < 64, below, above), 64, 1)
            sides.append(jnp.concatenate([top, bottom], axis=0))
        return halo_terms(1, primitives(*sides), side, 1, NZ)

    def add_y(to, edges):
        for f in range(5):
            edge = pltpu.roll(edges[f], 64, 1)
            to[f, :, 0:128] += jnp.where(lane_all < 64, edge, 0.0)
            to[f, :, 128:256] += jnp.where(lane_all >= 64, edge, 0.0)

    def add_x(to, f, term):
        to[f, 0:8] += jnp.where(row < 2, pltpu.roll(term, 2, 0), 0.0)
        to[f, 24:32] += jnp.where(row >= 6, pltpu.roll(term, 6, 0), 0.0)

    copies, up_copies = [], ()
    for tick in range(TICKS):
        now = u.at[tick]
        for f in range(5):
            first, last = now[f, :, 0:128], now[f, :, 128:256]
            y_send[tick, 0, f] = jnp.where(
                lane < 64, first[0:16], pltpu.roll(first[16:32], 64, 1)
            ).astype(jnp.bfloat16)
            y_send[tick, 1, f] = jnp.where(
                lane < 64, pltpu.roll(last[16:32], 64, 1), last[0:16]
            ).astype(jnp.bfloat16)
        if tick == 0:
            pl.semaphore_wait(
                barrier, 4 + 3 * has_up.astype(jnp.int32) + 3 * has_down.astype(jnp.int32)
            )
        to_y = (
            remote(y_send.at[tick, 0], y_hi.at[tick], y_ss.at[tick, 0], y_rs.at[tick, 0], {"gy": gy_down}),
            remote(y_send.at[tick, 1], y_lo.at[tick], y_ss.at[tick, 1], y_rs.at[tick, 1], {"gy": gy_up}),
        )
        to_x = (
            remote(now.at[:, 0:8], x_hi.at[tick], x_ss.at[tick, 0], x_rs.at[tick, 0], {"gx": gx_down}),
            remote(now.at[:, 24:32], x_lo.at[tick], x_ss.at[tick, 1], x_rs.at[tick, 1], {"gx": gx_up}),
        )
        diagonal = (
            remote(y_send.at[tick, 0], d_hi.at[tick], d_ss.at[tick, 0], d_rs.at[tick, 0], {"sec": sec_up, "gy": gy_down}),
            remote(y_send.at[tick, 1], d_lo.at[tick], d_ss.at[tick, 1], d_rs.at[tick, 1], {"sec": sec_up, "gy": gy_up}),
        )
        to_next = remote(
            f_send.at[tick], f_recv.at[tick], f_ss.at[tick], f_rs.at[tick], {"sec": sec_up}
        )
        x_next = remote(
            c_send.at[tick], c_recv.at[tick], c_ss.at[tick], c_rs.at[tick], {"sec": sec_up}
        )
        for copy in to_y + to_x:
            copy.start()

        @pl.when(has_up)
        def _():
            for copy in diagonal:
                copy.start()

        copies += to_y + to_x
        up_copies += (to_next, x_next) + diagonal

        for half in range(2):
            cols = slice(128 * half, 128 * half + 128)
            prims = primitives(*(now[f, :, cols] for f in range(5)))
            for f, term in enumerate(flux_difference(2, prims, z_difference)):
                rate[f, :, cols] = term
        main = primitives(*(now[f] for f in range(5)))
        for axis, array_axis, step in ((0, 0, 1), (1, 1, NZ)):
            zeros = jnp.zeros((8, 256) if axis == 0 else (32, 128), jnp.float32)
            ring = jax.tree.map(
                lambda v: jnp.concatenate([v, zeros], axis=array_axis), main
            )
            terms = flux_difference(axis, ring, ring_difference(array_axis, step))
            for f in range(5):
                total = rate[f] + terms[f][0:32, 0:256]
                rate[f] = total
                if axis == 1:
                    f_send[tick, f] = total.astype(jnp.bfloat16)

        @pl.when(has_up)
        def _():
            to_next.start()

        for copy in to_x:
            copy.wait_recv()
        prims = primitives(
            *(jnp.where(row < 4, x_hi[tick, f], x_lo[tick, f]) for f in range(5))
        )
        ends = halo_terms(0, prims, row, 0, 1)
        for pair in range(3):
            tile = ends[2 * pair]
            if pair < 2:
                inner = jnp.logical_and(row >= 2, row < 6)
                tile = jnp.where(inner, pltpu.roll(ends[2 * pair + 1], 4, 0), tile)
            c_send[tick, pair] = tile.astype(jnp.bfloat16)

        @pl.when(has_up)
        def _():
            x_next.start()

        for f in range(5):
            add_x(rate, f, ends[f])
        for copy in to_y:
            copy.wait_recv()
        add_y(rate, y_edges(y_lo[tick], y_hi[tick]))

        if tick == 0:
            load_st.wait()
        target = out.at[0] if tick == TICKS - 1 else u.at[tick + 1]

        @pl.when(level == 0)
        def _():
            for f in range(5):
                target[f] = now[f] + TIME_STEP * rate[f]

        @pl.when(has_down)
        def _():
            def past(h, f):
                return st[h, f].astype(jnp.float32) if h < 3 else past_fresh[h - 3, f]

            for f in range(5):
                known = W0 * past(tick, f) + W1 * past(tick + 1, f) + W2 * past(tick + 2, f)
                rate[f] = now[f] + TIME_STEP * (rate[f] + known)
            new = past_fresh.at[tick]
            for copy in diagonal:
                copy.wait_recv()
            edges = y_edges(d_lo[tick], d_hi[tick])
            for f in range(5):
                edge = pltpu.roll(edges[f], 64, 1)
                new[f, :, 0:128] = jnp.where(lane_all < 64, edge, 0.0)
                new[f, :, 128:256] = jnp.where(lane_all >= 64, edge, 0.0)
            to_next.wait_recv()
            for f in range(5):
                whole = new[f] + f_recv[tick, f].astype(jnp.float32)
                new[f] = whole
                target[f] = rate[f] + (TIME_STEP * W3) * whole
            x_next.wait_recv()
            for f in range(5):
                term = c_recv[tick, f // 2].astype(jnp.float32)
                if f % 2:
                    term = pltpu.roll(term, 4, 0)
                add_x(target, f, (TIME_STEP * W3) * term)
                add_x(new, f, term)

    @pl.when(has_up)
    def _():
        for copy in up_copies:
            copy.wait_send()

    for copy in copies:
        copy.wait_send()


def solution(mesh):
    counts = tuple(mesh.shape[name] for name in ("sec", "gx", "gy"))

    def per_device(fields, stored_rates):
        _, _, rows, cols = fields.shape
        halo_x = pltpu.VMEM((TICKS, 5, 8, cols), jnp.float32)
        halo_y = pltpu.VMEM((TICKS, 5, rows // 2, 128), jnp.bfloat16)
        block = (5, rows, cols)
        level_block = pltpu.VMEM((TICKS,) + block, jnp.bfloat16)
        x_terms = pltpu.VMEM((TICKS, 3, 8, cols), jnp.bfloat16)
        return pl.pallas_call(
            lambda *refs: kernel(counts, *refs),
            name="correct",
            out_shape=pltpu.VMEM(fields.shape, fields.dtype),
            in_specs=[pl.BlockSpec(memory_space=pl.ANY)] * 2,
            out_specs=pl.BlockSpec(memory_space=pltpu.VMEM),
            scratch_shapes=[
                pltpu.VMEM((TICKS,) + block, jnp.float32),
                pltpu.VMEM((3,) + block, jnp.bfloat16),
                pltpu.VMEM(block, jnp.float32),
                halo_x,
                halo_x,
                pltpu.VMEM((TICKS, 2, 5, rows // 2, 128), jnp.bfloat16),
                halo_y,
                halo_y,
                level_block,
                level_block,
                x_terms,
                x_terms,
                halo_y,
                halo_y,
                pltpu.VMEM((TICKS,) + block, jnp.float32),
                pltpu.SemaphoreType.DMA((2,)),
                pltpu.SemaphoreType.DMA((TICKS, 2)),
                pltpu.SemaphoreType.DMA((TICKS, 2)),
                pltpu.SemaphoreType.DMA((TICKS, 2)),
                pltpu.SemaphoreType.DMA((TICKS, 2)),
                pltpu.SemaphoreType.DMA((TICKS,)),
                pltpu.SemaphoreType.DMA((TICKS,)),
                pltpu.SemaphoreType.DMA((TICKS,)),
                pltpu.SemaphoreType.DMA((TICKS,)),
                pltpu.SemaphoreType.DMA((TICKS, 2)),
                pltpu.SemaphoreType.DMA((TICKS, 2)),
            ],
            compiler_params=pltpu.CompilerParams(collective_id=0, has_side_effects=True),
        )(fields, stored_rates)

    return jax.shard_map(
        per_device,
        mesh=mesh,
        in_specs=(P("sec", None, "gx", "gy"), P("sec", None, None, "gx", "gy")),
        out_specs=P("sec", None, "gx", "gy"),
        check_vma=False,
    )
```

```python
import jax
import jax.numpy as jnp
from jax import lax
from jax.experimental import pallas as pl
from jax.experimental.pallas import tpu as pltpu
from jax.sharding import PartitionSpec as P

NZ = 32
TICKS = 3
LEVELS = 4
TIME_STEP = 0.04
DYNAMIC_FRICTION = 0.4
CONDUCTIVITY = 0.5
GAMMA_LESS = 0.4
W0, W1, W2, W3 = 1.0 / 24.0, -5.0 / 24.0, 19.0 / 24.0 - 1.0, 9.0 / 24.0
MESH = pl.DeviceIdType.MESH


def primitives(density, mom_x, mom_y, mom_z, energy):
    inverse = 1.0 / density
    vel = (mom_x * inverse, mom_y * inverse, mom_z * inverse)
    kinetic = 0.5 * (vel[0] * vel[0] + vel[1] * vel[1] + vel[2] * vel[2])
    pressure = GAMMA_LESS * (energy - density * kinetic)
    heat = DYNAMIC_FRICTION * kinetic + CONDUCTIVITY * (pressure * inverse)
    return (mom_x, mom_y, mom_z), vel, pressure, energy + pressure, heat


def flux_difference(axis, prims, difference):
    mom, vel, pressure, enthalpy, heat = prims
    yield difference(mom[axis]) * -0.5
    for c in range(3):
        flux = mom[c] * vel[axis]
        if c == axis:
            flux = flux + pressure
        spread = difference(vel[c]) * (0.5 * DYNAMIC_FRICTION)
        yield difference(spread - flux) * 0.5
    spread = difference(heat) * 0.5
    yield difference(spread - enthalpy * vel[axis]) * 0.5


def ring_difference(axis, step):
    def difference(values):
        size = values.shape[axis]
        return pltpu.roll(values, size - step, axis) - pltpu.roll(values, step, axis)

    return difference


def z_difference(values):
    lane = lax.broadcasted_iota(jnp.int32, values.shape, 1) % NZ
    up = jnp.where(
        lane < NZ - 1, pltpu.roll(values, 127, 1), pltpu.roll(values, NZ - 1, 1)
    )
    down = jnp.where(lane > 0, pltpu.roll(values, 1, 1), pltpu.roll(values, 129 - NZ, 1))
    return up - down


def halo_terms(axis, prims, cell, array_axis, step):
    mom, vel, pressure, enthalpy, heat = prims
    size = cell.shape[array_axis]

    def outer(flux):
        after = pltpu.roll(flux, step, array_axis)
        before = pltpu.roll(flux, size - step, array_axis)
        return jnp.where(cell == 1, -0.5 * after, jnp.where(cell == 6, 0.5 * before, 0.0))

    terms = [outer(mom[axis])]
    for c in range(3):
        flux = mom[c] * vel[axis]
        if c == axis:
            flux = flux + pressure
        terms.append(outer(flux) + (0.25 * DYNAMIC_FRICTION) * vel[c])
    terms.append(outer(enthalpy * vel[axis]) + 0.25 * heat)
    return terms


def kernel(
    counts, fields, stored, out, u, st, rate, x_lo, x_hi, y_send, y_lo, y_hi,
    f_send, f_recv, c_send, c_recv, d_lo, d_hi, past_fresh,
    load_sem, x_ss, x_rs, y_ss, y_rs, f_ss, f_rs, c_ss, c_rs, d_ss, d_rs,
):
    n_sec, n_gx, n_gy = counts
    sec, gx, gy = lax.axis_index("sec"), lax.axis_index("gx"), lax.axis_index("gy")
    level = lax.rem(sec, LEVELS)
    gx_up, gx_down = lax.rem(gx + 1, n_gx), lax.rem(gx + n_gx - 1, n_gx)
    gy_up, gy_down = lax.rem(gy + 1, n_gy), lax.rem(gy + n_gy - 1, n_gy)
    sec_up, sec_down = lax.rem(sec + 1, n_sec), lax.rem(sec + n_sec - 1, n_sec)
    has_up, has_down = level < LEVELS - 1, level > 0

    load_u = pltpu.make_async_copy(fields.at[0], u.at[0], load_sem.at[0])
    load_st = pltpu.make_async_copy(stored.at[0], st, load_sem.at[1])
    load_u.start()
    load_st.start()

    barrier = pltpu.get_barrier_semaphore()
    @pl.when(has_up)
    def _():
        for target in ({"sec": sec_up}, {"sec": sec_up, "gy": gy_up}, {"sec": sec_up, "gy": gy_down}):
            pl.semaphore_signal(barrier, inc=1, device_id=target, device_id_type=MESH)

    @pl.when(has_down)
    def _():
        for target in ({"sec": sec_down}, {"sec": sec_down, "gy": gy_up}, {"sec": sec_down, "gy": gy_down}):
            pl.semaphore_signal(barrier, inc=1, device_id=target, device_id_type=MESH)

    for target in ({"gx": gx_up}, {"gx": gx_down}, {"gy": gy_up}, {"gy": gy_down}):
        pl.semaphore_signal(barrier, inc=1, device_id=target, device_id_type=MESH)

    load_u.wait()

    def remote(src, dst, send, recv, target):
        return pltpu.make_async_remote_copy(
            src_ref=src, dst_ref=dst, send_sem=send, recv_sem=recv,
            device_id=target, device_id_type=MESH,
        )

    lane = lax.broadcasted_iota(jnp.int32, (16, 128), 1)
    row = lax.broadcasted_iota(jnp.int32, (8, 256), 0)
    lane_all = lax.broadcasted_iota(jnp.int32, (32, 128), 1)
    side = lane_all // NZ
    side = jnp.where(side < 2, side, side + 4)

    def y_edges(low, high):
        sides = []
        for f in range(5):
            above, below = high[f].astype(jnp.float32), low[f].astype(jnp.float32)
            top = jnp.where(lane < 64, above, below)
            bottom = pltpu.roll(jnp.where(lane < 64, below, above), 64, 1)
            sides.append(jnp.concatenate([top, bottom], axis=0))
        return halo_terms(1, primitives(*sides), side, 1, NZ)

    def add_y(to, edges):
        for f in range(5):
            edge = pltpu.roll(edges[f], 64, 1)
            to[f, :, 0:128] += jnp.where(lane_all < 64, edge, 0.0)
            to[f, :, 128:256] += jnp.where(lane_all >= 64, edge, 0.0)

    def add_x(to, f, term):
        to[f, 0:8] += jnp.where(row < 2, pltpu.roll(term, 2, 0), 0.0)
        to[f, 24:32] += jnp.where(row >= 6, pltpu.roll(term, 6, 0), 0.0)

    copies, up_copies = [], ()
    for tick in range(TICKS):
        now = u.at[tick]
        for f in range(5):
            first, last = now[f, :, 0:128], now[f, :, 128:256]
            y_send[tick, 0, f] = jnp.where(
                lane < 64, first[0:16], pltpu.roll(first[16:32], 64, 1)
            ).astype(jnp.bfloat16)
            y_send[tick, 1, f] = jnp.where(
                lane < 64, pltpu.roll(last[16:32], 64, 1), last[0:16]
            ).astype(jnp.bfloat16)
        if tick == 0:
            pl.semaphore_wait(
                barrier, 4 + 3 * has_up.astype(jnp.int32) + 3 * has_down.astype(jnp.int32)
            )
        to_y = (
            remote(y_send.at[tick, 0], y_hi.at[tick], y_ss.at[tick, 0], y_rs.at[tick, 0], {"gy": gy_down}),
            remote(y_send.at[tick, 1], y_lo.at[tick], y_ss.at[tick, 1], y_rs.at[tick, 1], {"gy": gy_up}),
        )
        to_x = (
            remote(now.at[:, 0:8], x_hi.at[tick], x_ss.at[tick, 0], x_rs.at[tick, 0], {"gx": gx_down}),
            remote(now.at[:, 24:32], x_lo.at[tick], x_ss.at[tick, 1], x_rs.at[tick, 1], {"gx": gx_up}),
        )
        diagonal = (
            remote(y_send.at[tick, 0], d_hi.at[tick], d_ss.at[tick, 0], d_rs.at[tick, 0], {"sec": sec_up, "gy": gy_down}),
            remote(y_send.at[tick, 1], d_lo.at[tick], d_ss.at[tick, 1], d_rs.at[tick, 1], {"sec": sec_up, "gy": gy_up}),
        )
        to_next = tuple(
            remote(
                f_send.at[tick, f], f_recv.at[tick, f], f_ss.at[tick, f], f_rs.at[tick, f],
                {"sec": sec_up},
            )
            for f in range(5)
        )
        x_next = remote(
            c_send.at[tick], c_recv.at[tick], c_ss.at[tick], c_rs.at[tick], {"sec": sec_up}
        )
        @pl.when(has_up)
        def _():
            for copy in diagonal:
                copy.start()

        for copy in to_y + to_x:
            copy.start()

        copies += to_y + to_x
        up_copies += to_next + (x_next,) + diagonal

        for half in range(2):
            cols = slice(128 * half, 128 * half + 128)
            prims = primitives(*(now[f, :, cols] for f in range(5)))
            for f, term in enumerate(flux_difference(2, prims, z_difference)):
                rate[f, :, cols] = term
        main = primitives(*(now[f] for f in range(5)))
        for axis, array_axis, step in ((0, 0, 1), (1, 1, NZ)):
            zeros = jnp.zeros((8, 256) if axis == 0 else (32, 128), jnp.float32)
            ring = jax.tree.map(
                lambda v: jnp.concatenate([v, zeros], axis=array_axis), main
            )
            terms = flux_difference(axis, ring, ring_difference(array_axis, step))
            for f, term in enumerate(terms):
                total = rate[f] + term[0:32, 0:256]
                rate[f] = total
                if axis == 1:
                    f_send[tick, f] = total.astype(jnp.bfloat16)
                    pl.when(has_up)(to_next[f].start)

        for copy in to_x:
            copy.wait_recv()
        prims = primitives(
            *(jnp.where(row < 4, x_hi[tick, f], x_lo[tick, f]) for f in range(5))
        )
        ends = halo_terms(0, prims, row, 0, 1)
        for pair in range(3):
            tile = ends[2 * pair]
            if pair < 2:
                inner = jnp.logical_and(row >= 2, row < 6)
                tile = jnp.where(inner, pltpu.roll(ends[2 * pair + 1], 4, 0), tile)
            c_send[tick, pair] = tile.astype(jnp.bfloat16)

        @pl.when(has_up)
        def _():
            x_next.start()

        for f in range(5):
            add_x(rate, f, ends[f])
        for copy in to_y:
            copy.wait_recv()
        add_y(rate, y_edges(y_lo[tick], y_hi[tick]))

        if tick == 0:
            load_st.wait()
        target = out.at[0] if tick == TICKS - 1 else u.at[tick + 1]

        @pl.when(level == 0)
        def _():
            for f in range(5):
                target[f] = now[f] + TIME_STEP * rate[f]

        @pl.when(has_down)
        def _():
            def past(h, f):
                return st[h, f].astype(jnp.float32) if h < 3 else past_fresh[h - 3, f]

            for f in range(5):
                known = W0 * past(tick, f) + W1 * past(tick + 1, f) + W2 * past(tick + 2, f)
                rate[f] = now[f] + TIME_STEP * (rate[f] + known)
            new = past_fresh.at[tick]
            for copy in diagonal:
                copy.wait_recv()
            edges = y_edges(d_lo[tick], d_hi[tick])
            for f in range(5):
                edge = pltpu.roll(edges[f], 64, 1)
                new[f, :, 0:128] = jnp.where(lane_all < 64, edge, 0.0)
                new[f, :, 128:256] = jnp.where(lane_all >= 64, edge, 0.0)
            for f in range(5):
                to_next[f].wait_recv()
                whole = new[f] + f_recv[tick, f].astype(jnp.float32)
                new[f] = whole
                target[f] = rate[f] + (TIME_STEP * W3) * whole
            x_next.wait_recv()
            for f in range(5):
                term = c_recv[tick, f // 2].astype(jnp.float32)
                if f % 2:
                    term = pltpu.roll(term, 4, 0)
                add_x(target, f, (TIME_STEP * W3) * term)
                add_x(new, f, term)

    @pl.when(has_up)
    def _():
        for copy in up_copies:
            copy.wait_send()

    for copy in copies:
        copy.wait_send()


def solution(mesh):
    counts = tuple(mesh.shape[name] for name in ("sec", "gx", "gy"))

    def per_device(fields, stored_rates):
        _, _, rows, cols = fields.shape
        halo_x = pltpu.VMEM((TICKS, 5, 8, cols), jnp.float32)
        halo_y = pltpu.VMEM((TICKS, 5, rows // 2, 128), jnp.bfloat16)
        block = (5, rows, cols)
        level_block = pltpu.VMEM((TICKS,) + block, jnp.bfloat16)
        x_terms = pltpu.VMEM((TICKS, 3, 8, cols), jnp.bfloat16)
        return pl.pallas_call(
            lambda *refs: kernel(counts, *refs),
            name="correct",
            out_shape=pltpu.VMEM(fields.shape, fields.dtype),
            in_specs=[pl.BlockSpec(memory_space=pl.ANY)] * 2,
            out_specs=pl.BlockSpec(memory_space=pltpu.VMEM),
            scratch_shapes=[
                pltpu.VMEM((TICKS,) + block, jnp.float32),
                pltpu.VMEM((3,) + block, jnp.bfloat16),
                pltpu.VMEM(block, jnp.float32),
                halo_x,
                halo_x,
                pltpu.VMEM((TICKS, 2, 5, rows // 2, 128), jnp.bfloat16),
                halo_y,
                halo_y,
                level_block,
                level_block,
                x_terms,
                x_terms,
                halo_y,
                halo_y,
                pltpu.VMEM((TICKS,) + block, jnp.float32),
                pltpu.SemaphoreType.DMA((2,)),
                pltpu.SemaphoreType.DMA((TICKS, 2)),
                pltpu.SemaphoreType.DMA((TICKS, 2)),
                pltpu.SemaphoreType.DMA((TICKS, 2)),
                pltpu.SemaphoreType.DMA((TICKS, 2)),
                pltpu.SemaphoreType.DMA((TICKS, 5)),
                pltpu.SemaphoreType.DMA((TICKS, 5)),
                pltpu.SemaphoreType.DMA((TICKS,)),
                pltpu.SemaphoreType.DMA((TICKS,)),
                pltpu.SemaphoreType.DMA((TICKS, 2)),
                pltpu.SemaphoreType.DMA((TICKS, 2)),
            ],
            compiler_params=pltpu.CompilerParams(collective_id=0, has_side_effects=True),
        )(fields, stored_rates)

    return jax.shard_map(
        per_device,
        mesh=mesh,
        in_specs=(P("sec", None, "gx", "gy"), P("sec", None, None, "gx", "gy")),
        out_specs=P("sec", None, "gx", "gy"),
        check_vma=False,
    )
```

```python
import jax
import jax.numpy as jnp
from jax import lax
from jax.experimental import pallas as pl
from jax.experimental.pallas import tpu as pltpu
from jax.sharding import PartitionSpec as P

NZ = 32
TICKS = 3
LEVELS = 4
TIME_STEP = 0.04
DYNAMIC_FRICTION = 0.4
CONDUCTIVITY = 0.5
GAMMA_LESS = 0.4
W0, W1, W2, W3 = 1.0 / 24.0, -5.0 / 24.0, 19.0 / 24.0 - 1.0, 9.0 / 24.0
MESH = pl.DeviceIdType.MESH


def primitives(density, mom_x, mom_y, mom_z, energy):
    inverse = 1.0 / density
    vel = (mom_x * inverse, mom_y * inverse, mom_z * inverse)
    kinetic = 0.5 * (vel[0] * vel[0] + vel[1] * vel[1] + vel[2] * vel[2])
    pressure = GAMMA_LESS * (energy - density * kinetic)
    heat = DYNAMIC_FRICTION * kinetic + CONDUCTIVITY * (pressure * inverse)
    return (mom_x, mom_y, mom_z), vel, pressure, energy + pressure, heat


def flux_difference(axis, prims, difference):
    mom, vel, pressure, enthalpy, heat = prims
    yield difference(mom[axis]) * -0.5
    for c in range(3):
        flux = mom[c] * vel[axis]
        if c == axis:
            flux = flux + pressure
        spread = difference(vel[c]) * (0.5 * DYNAMIC_FRICTION)
        yield difference(spread - flux) * 0.5
    spread = difference(heat) * 0.5
    yield difference(spread - enthalpy * vel[axis]) * 0.5


def ring_difference(axis, step):
    def difference(values):
        size = values.shape[axis]
        return pltpu.roll(values, size - step, axis) - pltpu.roll(values, step, axis)

    return difference


def z_difference(values):
    lane = lax.broadcasted_iota(jnp.int32, values.shape, 1) % NZ
    up = jnp.where(
        lane < NZ - 1, pltpu.roll(values, 127, 1), pltpu.roll(values, NZ - 1, 1)
    )
    down = jnp.where(lane > 0, pltpu.roll(values, 1, 1), pltpu.roll(values, 129 - NZ, 1))
    return up - down


def halo_terms(axis, prims, cell, array_axis, step):
    mom, vel, pressure, enthalpy, heat = prims
    size = cell.shape[array_axis]

    def outer(flux):
        after = pltpu.roll(flux, step, array_axis)
        before = pltpu.roll(flux, size - step, array_axis)
        return jnp.where(cell == 1, -0.5 * after, jnp.where(cell == 6, 0.5 * before, 0.0))

    terms = [outer(mom[axis])]
    for c in range(3):
        flux = mom[c] * vel[axis]
        if c == axis:
            flux = flux + pressure
        terms.append(outer(flux) + (0.25 * DYNAMIC_FRICTION) * vel[c])
    terms.append(outer(enthalpy * vel[axis]) + 0.25 * heat)
    return terms


def kernel(
    counts, fields, stored, out, u, st, rate, x_lo, x_hi, y_send, y_lo, y_hi,
    f_send, f_recv, c_send, c_recv, d_lo, d_hi, past_fresh,
    load_sem, x_ss, x_rs, y_ss, y_rs, f_ss, f_rs, c_ss, c_rs, d_ss, d_rs,
):
    n_sec, n_gx, n_gy = counts
    sec, gx, gy = lax.axis_index("sec"), lax.axis_index("gx"), lax.axis_index("gy")
    level = lax.rem(sec, LEVELS)
    gx_up, gx_down = lax.rem(gx + 1, n_gx), lax.rem(gx + n_gx - 1, n_gx)
    gy_up, gy_down = lax.rem(gy + 1, n_gy), lax.rem(gy + n_gy - 1, n_gy)
    sec_up, sec_down = lax.rem(sec + 1, n_sec), lax.rem(sec + n_sec - 1, n_sec)
    has_up, has_down = level < LEVELS - 1, level > 0

    load_u = pltpu.make_async_copy(fields.at[0], u.at[0], load_sem.at[0])
    load_st = pltpu.make_async_copy(stored.at[0], st, load_sem.at[1])
    load_u.start()
    load_st.start()

    barrier = pltpu.get_barrier_semaphore()
    @pl.when(has_up)
    def _():
        for target in ({"sec": sec_up}, {"sec": sec_up, "gy": gy_up}, {"sec": sec_up, "gy": gy_down}):
            pl.semaphore_signal(barrier, inc=1, device_id=target, device_id_type=MESH)

    @pl.when(has_down)
    def _():
        for target in ({"sec": sec_down}, {"sec": sec_down, "gy": gy_up}, {"sec": sec_down, "gy": gy_down}):
            pl.semaphore_signal(barrier, inc=1, device_id=target, device_id_type=MESH)

    for target in ({"gx": gx_up}, {"gx": gx_down}, {"gy": gy_up}, {"gy": gy_down}):
        pl.semaphore_signal(barrier, inc=1, device_id=target, device_id_type=MESH)

    load_u.wait()

    def remote(src, dst, send, recv, target):
        return pltpu.make_async_remote_copy(
            src_ref=src, dst_ref=dst, send_sem=send, recv_sem=recv,
            device_id=target, device_id_type=MESH,
        )

    lane = lax.broadcasted_iota(jnp.int32, (16, 128), 1)
    row = lax.broadcasted_iota(jnp.int32, (8, 256), 0)
    lane_all = lax.broadcasted_iota(jnp.int32, (32, 128), 1)
    side = lane_all // NZ
    side = jnp.where(side < 2, side, side + 4)

    def y_edges(low, high):
        sides = []
        for f in range(5):
            above, below = high[f].astype(jnp.float32), low[f].astype(jnp.float32)
            top = jnp.where(lane < 64, above, below)
            bottom = pltpu.roll(jnp.where(lane < 64, below, above), 64, 1)
            sides.append(jnp.concatenate([top, bottom], axis=0))
        return halo_terms(1, primitives(*sides), side, 1, NZ)

    def add_y(to, edges):
        for f in range(5):
            edge = pltpu.roll(edges[f], 64, 1)
            to[f, :, 0:128] += jnp.where(lane_all < 64, edge, 0.0)
            to[f, :, 128:256] += jnp.where(lane_all >= 64, edge, 0.0)

    def add_x(to, f, term):
        to[f, 0:8] += jnp.where(row < 2, pltpu.roll(term, 2, 0), 0.0)
        to[f, 24:32] += jnp.where(row >= 6, pltpu.roll(term, 6, 0), 0.0)

    copies, up_copies = [], ()
    for tick in range(TICKS):
        now = u.at[tick]
        for f in range(5):
            first, last = now[f, :, 0:128], now[f, :, 128:256]
            y_send[tick, 0, f] = jnp.where(
                lane < 64, first[0:16], pltpu.roll(first[16:32], 64, 1)
            ).astype(jnp.bfloat16)
            y_send[tick, 1, f] = jnp.where(
                lane < 64, pltpu.roll(last[16:32], 64, 1), last[0:16]
            ).astype(jnp.bfloat16)
        if tick == 0:
            pl.semaphore_wait(
                barrier, 4 + 3 * has_up.astype(jnp.int32) + 3 * has_down.astype(jnp.int32)
            )
        to_y = (
            remote(y_send.at[tick, 0], y_hi.at[tick], y_ss.at[tick, 0], y_rs.at[tick, 0], {"gy": gy_down}),
            remote(y_send.at[tick, 1], y_lo.at[tick], y_ss.at[tick, 1], y_rs.at[tick, 1], {"gy": gy_up}),
        )
        to_x = (
            remote(now.at[:, 0:8], x_hi.at[tick], x_ss.at[tick, 0], x_rs.at[tick, 0], {"gx": gx_down}),
            remote(now.at[:, 24:32], x_lo.at[tick], x_ss.at[tick, 1], x_rs.at[tick, 1], {"gx": gx_up}),
        )
        diagonal = (
            remote(y_send.at[tick, 0], d_hi.at[tick], d_ss.at[tick, 0], d_rs.at[tick, 0], {"sec": sec_up, "gy": gy_down}),
            remote(y_send.at[tick, 1], d_lo.at[tick], d_ss.at[tick, 1], d_rs.at[tick, 1], {"sec": sec_up, "gy": gy_up}),
        )
        to_next = tuple(
            remote(
                f_send.at[tick, f], f_recv.at[tick, f], f_ss.at[tick, f], f_rs.at[tick, f],
                {"sec": sec_up},
            )
            for f in range(5)
        )
        x_next = remote(
            c_send.at[tick], c_recv.at[tick], c_ss.at[tick], c_rs.at[tick], {"sec": sec_up}
        )
        @pl.when(has_up)
        def _():
            for copy in diagonal:
                copy.start()

        for copy in to_y + to_x:
            copy.start()

        copies += to_y + to_x
        up_copies += to_next + (x_next,) + diagonal

        for half in range(2):
            cols = slice(128 * half, 128 * half + 128)
            prims = primitives(*(now[f, :, cols] for f in range(5)))
            for f, term in enumerate(flux_difference(2, prims, z_difference)):
                rate[f, :, cols] = term
        main = primitives(*(now[f] for f in range(5)))
        for axis, array_axis, step in ((0, 0, 1), (1, 1, NZ)):
            zeros = jnp.zeros((8, 256) if axis == 0 else (32, 128), jnp.float32)
            ring = jax.tree.map(
                lambda v: jnp.concatenate([v, zeros], axis=array_axis), main
            )
            terms = flux_difference(axis, ring, ring_difference(array_axis, step))
            for f, term in enumerate(terms):
                total = rate[f] + term[0:32, 0:256]
                rate[f] = total
                if axis == 1:
                    f_send[tick, f] = total.astype(jnp.bfloat16)
                    pl.when(has_up)(to_next[f].start)

        for copy in to_x:
            copy.wait_recv()
        prims = primitives(
            *(jnp.where(row < 4, x_hi[tick, f], x_lo[tick, f]) for f in range(5))
        )
        ends = halo_terms(0, prims, row, 0, 1)
        for pair in range(3):
            tile = ends[2 * pair]
            if pair < 2:
                inner = jnp.logical_and(row >= 2, row < 6)
                tile = jnp.where(inner, pltpu.roll(ends[2 * pair + 1], 4, 0), tile)
            c_send[tick, pair] = tile.astype(jnp.bfloat16)

        @pl.when(has_up)
        def _():
            x_next.start()

        for f in range(5):
            add_x(rate, f, ends[f])
        for copy in to_y:
            copy.wait_recv()
        add_y(rate, y_edges(y_lo[tick], y_hi[tick]))

        if tick == 0:
            load_st.wait()
        target = out.at[0] if tick == TICKS - 1 else u.at[tick + 1]

        @pl.when(level == 0)
        def _():
            for f in range(5):
                target[f] = now[f] + TIME_STEP * rate[f]

        @pl.when(has_down)
        def _():
            def past(h, f):
                return st[h, f].astype(jnp.float32) if h < 3 else past_fresh[h - 3, f]

            for f in range(5):
                known = W0 * past(tick, f) + W1 * past(tick + 1, f) + W2 * past(tick + 2, f)
                rate[f] = now[f] + TIME_STEP * (rate[f] + known)
            new = past_fresh.at[tick]
            for f in range(5):
                to_next[f].wait_recv()
                whole = f_recv[tick, f].astype(jnp.float32)
                new[f] = whole
                target[f] = rate[f] + (TIME_STEP * W3) * whole
            x_next.wait_recv()
            for f in range(5):
                term = c_recv[tick, f // 2].astype(jnp.float32)
                if f % 2:
                    term = pltpu.roll(term, 4, 0)
                add_x(target, f, (TIME_STEP * W3) * term)
                add_x(new, f, term)
            for copy in diagonal:
                copy.wait_recv()
            edges = y_edges(d_lo[tick], d_hi[tick])
            add_y(target, [(TIME_STEP * W3) * edge for edge in edges])
            if tick < TICKS - 1:
                add_y(new, edges)

    @pl.when(has_up)
    def _():
        for copy in up_copies:
            copy.wait_send()

    for copy in copies:
        copy.wait_send()


def solution(mesh):
    counts = tuple(mesh.shape[name] for name in ("sec", "gx", "gy"))

    def per_device(fields, stored_rates):
        _, _, rows, cols = fields.shape
        halo_x = pltpu.VMEM((TICKS, 5, 8, cols), jnp.float32)
        halo_y = pltpu.VMEM((TICKS, 5, rows // 2, 128), jnp.bfloat16)
        block = (5, rows, cols)
        level_block = pltpu.VMEM((TICKS,) + block, jnp.bfloat16)
        x_terms = pltpu.VMEM((TICKS, 3, 8, cols), jnp.bfloat16)
        return pl.pallas_call(
            lambda *refs: kernel(counts, *refs),
            name="correct",
            out_shape=pltpu.VMEM(fields.shape, fields.dtype),
            in_specs=[pl.BlockSpec(memory_space=pl.ANY)] * 2,
            out_specs=pl.BlockSpec(memory_space=pltpu.VMEM),
            scratch_shapes=[
                pltpu.VMEM((TICKS,) + block, jnp.float32),
                pltpu.VMEM((3,) + block, jnp.bfloat16),
                pltpu.VMEM(block, jnp.float32),
                halo_x,
                halo_x,
                pltpu.VMEM((TICKS, 2, 5, rows // 2, 128), jnp.bfloat16),
                halo_y,
                halo_y,
                level_block,
                level_block,
                x_terms,
                x_terms,
                halo_y,
                halo_y,
                pltpu.VMEM((TICKS,) + block, jnp.float32),
                pltpu.SemaphoreType.DMA((2,)),
                pltpu.SemaphoreType.DMA((TICKS, 2)),
                pltpu.SemaphoreType.DMA((TICKS, 2)),
                pltpu.SemaphoreType.DMA((TICKS, 2)),
                pltpu.SemaphoreType.DMA((TICKS, 2)),
                pltpu.SemaphoreType.DMA((TICKS, 5)),
                pltpu.SemaphoreType.DMA((TICKS, 5)),
                pltpu.SemaphoreType.DMA((TICKS,)),
                pltpu.SemaphoreType.DMA((TICKS,)),
                pltpu.SemaphoreType.DMA((TICKS, 2)),
                pltpu.SemaphoreType.DMA((TICKS, 2)),
            ],
            compiler_params=pltpu.CompilerParams(collective_id=0, has_side_effects=True),
        )(fields, stored_rates)

    return jax.shard_map(
        per_device,
        mesh=mesh,
        in_specs=(P("sec", None, "gx", "gy"), P("sec", None, None, "gx", "gy")),
        out_specs=P("sec", None, "gx", "gy"),
        check_vma=False,
    )
```

```python
import jax
import jax.numpy as jnp
from jax import lax
from jax.experimental import pallas as pl
from jax.experimental.pallas import tpu as pltpu
from jax.sharding import PartitionSpec as P

NZ = 32
TICKS = 3
LEVELS = 4
TIME_STEP = 0.04
DYNAMIC_FRICTION = 0.4
CONDUCTIVITY = 0.5
GAMMA_LESS = 0.4
W0, W1, W2, W3 = 1.0 / 24.0, -5.0 / 24.0, 19.0 / 24.0 - 1.0, 9.0 / 24.0
MESH = pl.DeviceIdType.MESH


def primitives(density, mom_x, mom_y, mom_z, energy):
    inverse = 1.0 / density
    vel = (mom_x * inverse, mom_y * inverse, mom_z * inverse)
    kinetic = 0.5 * (vel[0] * vel[0] + vel[1] * vel[1] + vel[2] * vel[2])
    pressure = GAMMA_LESS * (energy - density * kinetic)
    heat = DYNAMIC_FRICTION * kinetic + CONDUCTIVITY * (pressure * inverse)
    return (mom_x, mom_y, mom_z), vel, pressure, energy + pressure, heat


def flux_difference(axis, prims, difference):
    mom, vel, pressure, enthalpy, heat = prims
    yield difference(mom[axis]) * -0.5
    for c in range(3):
        flux = mom[c] * vel[axis]
        if c == axis:
            flux = flux + pressure
        spread = difference(vel[c]) * (0.5 * DYNAMIC_FRICTION)
        yield difference(spread - flux) * 0.5
    spread = difference(heat) * 0.5
    yield difference(spread - enthalpy * vel[axis]) * 0.5


def ring_difference(axis, step):
    def difference(values):
        size = values.shape[axis]
        return pltpu.roll(values, size - step, axis) - pltpu.roll(values, step, axis)

    return difference


def z_difference(values):
    lane = lax.broadcasted_iota(jnp.int32, values.shape, 1) % NZ
    up = jnp.where(
        lane < NZ - 1, pltpu.roll(values, 127, 1), pltpu.roll(values, NZ - 1, 1)
    )
    down = jnp.where(lane > 0, pltpu.roll(values, 1, 1), pltpu.roll(values, 129 - NZ, 1))
    return up - down


def halo_terms(axis, prims, cell, array_axis, step):
    mom, vel, pressure, enthalpy, heat = prims
    size = cell.shape[array_axis]

    def outer(flux):
        after = pltpu.roll(flux, step, array_axis)
        before = pltpu.roll(flux, size - step, array_axis)
        return jnp.where(cell == 1, -0.5 * after, jnp.where(cell == 6, 0.5 * before, 0.0))

    terms = [outer(mom[axis])]
    for c in range(3):
        flux = mom[c] * vel[axis]
        if c == axis:
            flux = flux + pressure
        terms.append(outer(flux) + (0.25 * DYNAMIC_FRICTION) * vel[c])
    terms.append(outer(enthalpy * vel[axis]) + 0.25 * heat)
    return terms


def kernel(
    counts, fields, stored, out, u, st, rate, x_lo, x_hi, y_send, y_lo, y_hi,
    f_send, f_recv, c_send, c_recv, d_lo, d_hi, past_fresh,
    load_sem, x_ss, x_rs, y_ss, y_rs, f_ss, f_rs, c_ss, c_rs, d_ss, d_rs,
):
    n_sec, n_gx, n_gy = counts
    sec, gx, gy = lax.axis_index("sec"), lax.axis_index("gx"), lax.axis_index("gy")
    level = lax.rem(sec, LEVELS)
    gx_up, gx_down = lax.rem(gx + 1, n_gx), lax.rem(gx + n_gx - 1, n_gx)
    gy_up, gy_down = lax.rem(gy + 1, n_gy), lax.rem(gy + n_gy - 1, n_gy)
    sec_up, sec_down = lax.rem(sec + 1, n_sec), lax.rem(sec + n_sec - 1, n_sec)
    has_up, has_down = level < LEVELS - 1, level > 0

    load_u = pltpu.make_async_copy(fields.at[0], u.at[0], load_sem.at[0])
    load_st = pltpu.make_async_copy(stored.at[0], st, load_sem.at[1])
    load_u.start()
    load_st.start()

    barrier = pltpu.get_barrier_semaphore()
    @pl.when(has_up)
    def _():
        for target in ({"sec": sec_up}, {"sec": sec_up, "gy": gy_up}, {"sec": sec_up, "gy": gy_down}):
            pl.semaphore_signal(barrier, inc=1, device_id=target, device_id_type=MESH)

    @pl.when(has_down)
    def _():
        for target in ({"sec": sec_down}, {"sec": sec_down, "gy": gy_up}, {"sec": sec_down, "gy": gy_down}):
            pl.semaphore_signal(barrier, inc=1, device_id=target, device_id_type=MESH)

    for target in ({"gx": gx_up}, {"gx": gx_down}, {"gy": gy_up}, {"gy": gy_down}):
        pl.semaphore_signal(barrier, inc=1, device_id=target, device_id_type=MESH)

    load_u.wait()

    def remote(src, dst, send, recv, target):
        return pltpu.make_async_remote_copy(
            src_ref=src, dst_ref=dst, send_sem=send, recv_sem=recv,
            device_id=target, device_id_type=MESH,
        )

    lane = lax.broadcasted_iota(jnp.int32, (16, 128), 1)
    row = lax.broadcasted_iota(jnp.int32, (8, 256), 0)
    lane_all = lax.broadcasted_iota(jnp.int32, (32, 128), 1)
    side = lane_all // NZ
    side = jnp.where(side < 2, side, side + 4)

    def y_edges(low, high):
        sides = []
        for f in range(5):
            above, below = high[f].astype(jnp.float32), low[f].astype(jnp.float32)
            top = jnp.where(lane < 64, above, below)
            bottom = pltpu.roll(jnp.where(lane < 64, below, above), 64, 1)
            sides.append(jnp.concatenate([top, bottom], axis=0))
        return halo_terms(1, primitives(*sides), side, 1, NZ)

    def add_y(to, edges):
        for f in range(5):
            edge = pltpu.roll(edges[f], 64, 1)
            to[f, :, 0:128] += jnp.where(lane_all < 64, edge, 0.0)
            to[f, :, 128:256] += jnp.where(lane_all >= 64, edge, 0.0)

    def add_x(to, f, term):
        to[f, 0:8] += jnp.where(row < 2, pltpu.roll(term, 2, 0), 0.0)
        to[f, 24:32] += jnp.where(row >= 6, pltpu.roll(term, 6, 0), 0.0)

    copies, up_copies = [], ()
    for tick in range(TICKS):
        now = u.at[tick]
        to_x = (
            remote(now.at[:, 0:8], x_hi.at[tick], x_ss.at[tick, 0], x_rs.at[tick, 0], {"gx": gx_down}),
            remote(now.at[:, 24:32], x_lo.at[tick], x_ss.at[tick, 1], x_rs.at[tick, 1], {"gx": gx_up}),
        )
        if tick > 0:
            for copy in to_x:
                copy.start()
        for f in range(5):
            first, last = now[f, :, 0:128], now[f, :, 128:256]
            y_send[tick, 0, f] = jnp.where(
                lane < 64, first[0:16], pltpu.roll(first[16:32], 64, 1)
            ).astype(jnp.bfloat16)
            y_send[tick, 1, f] = jnp.where(
                lane < 64, pltpu.roll(last[16:32], 64, 1), last[0:16]
            ).astype(jnp.bfloat16)
        if tick == 0:
            pl.semaphore_wait(
                barrier, 4 + 3 * has_up.astype(jnp.int32) + 3 * has_down.astype(jnp.int32)
            )
        to_y = (
            remote(y_send.at[tick, 0], y_hi.at[tick], y_ss.at[tick, 0], y_rs.at[tick, 0], {"gy": gy_down}),
            remote(y_send.at[tick, 1], y_lo.at[tick], y_ss.at[tick, 1], y_rs.at[tick, 1], {"gy": gy_up}),
        )
        diagonal = (
            remote(y_send.at[tick, 0], d_hi.at[tick], d_ss.at[tick, 0], d_rs.at[tick, 0], {"sec": sec_up, "gy": gy_down}),
            remote(y_send.at[tick, 1], d_lo.at[tick], d_ss.at[tick, 1], d_rs.at[tick, 1], {"sec": sec_up, "gy": gy_up}),
        )
        to_next = tuple(
            remote(
                f_send.at[tick, f], f_recv.at[tick, f], f_ss.at[tick, f], f_rs.at[tick, f],
                {"sec": sec_up},
            )
            for f in range(5)
        )
        x_next = remote(
            c_send.at[tick], c_recv.at[tick], c_ss.at[tick], c_rs.at[tick], {"sec": sec_up}
        )
        @pl.when(has_up)
        def _():
            for copy in diagonal:
                copy.start()

        for copy in to_y + (to_x if tick == 0 else ()):
            copy.start()

        copies += to_y + to_x
        up_copies += to_next + (x_next,) + diagonal

        for half in range(2):
            cols = slice(128 * half, 128 * half + 128)
            prims = primitives(*(now[f, :, cols] for f in range(5)))
            for f, term in enumerate(flux_difference(2, prims, z_difference)):
                rate[f, :, cols] = term
        main = primitives(*(now[f] for f in range(5)))
        for axis, array_axis, step in ((0, 0, 1), (1, 1, NZ)):
            zeros = jnp.zeros((8, 256) if axis == 0 else (32, 128), jnp.float32)
            ring = jax.tree.map(
                lambda v: jnp.concatenate([v, zeros], axis=array_axis), main
            )
            terms = flux_difference(axis, ring, ring_difference(array_axis, step))
            for f, term in enumerate(terms):
                total = rate[f] + term[0:32, 0:256]
                rate[f] = total
                if axis == 1:
                    f_send[tick, f] = total.astype(jnp.bfloat16)
                    pl.when(has_up)(to_next[f].start)

        for copy in to_x:
            copy.wait_recv()
        prims = primitives(
            *(jnp.where(row < 4, x_hi[tick, f], x_lo[tick, f]) for f in range(5))
        )
        ends = halo_terms(0, prims, row, 0, 1)
        for pair in range(3):
            tile = ends[2 * pair]
            if pair < 2:
                inner = jnp.logical_and(row >= 2, row < 6)
                tile = jnp.where(inner, pltpu.roll(ends[2 * pair + 1], 4, 0), tile)
            c_send[tick, pair] = tile.astype(jnp.bfloat16)

        @pl.when(has_up)
        def _():
            x_next.start()

        for f in range(5):
            add_x(rate, f, ends[f])
        for copy in to_y:
            copy.wait_recv()
        add_y(rate, y_edges(y_lo[tick], y_hi[tick]))

        if tick == 0:
            load_st.wait()
        target = out.at[0] if tick == TICKS - 1 else u.at[tick + 1]

        @pl.when(level == 0)
        def _():
            for f in range(5):
                target[f] = now[f] + TIME_STEP * rate[f]

        @pl.when(has_down)
        def _():
            def past(h, f):
                return st[h, f].astype(jnp.float32) if h < 3 else past_fresh[h - 3, f]

            for f in range(5):
                known = W0 * past(tick, f) + W1 * past(tick + 1, f) + W2 * past(tick + 2, f)
                rate[f] = now[f] + TIME_STEP * (rate[f] + known)
            new = past_fresh.at[tick]
            for copy in diagonal:
                copy.wait_recv()
            edges = y_edges(d_lo[tick], d_hi[tick])
            for f in range(5):
                edge = pltpu.roll(edges[f], 64, 1)
                new[f, :, 0:128] = jnp.where(lane_all < 64, edge, 0.0)
                new[f, :, 128:256] = jnp.where(lane_all >= 64, edge, 0.0)
            for f in range(5):
                to_next[f].wait_recv()
                whole = new[f] + f_recv[tick, f].astype(jnp.float32)
                new[f] = whole
                target[f] = rate[f] + (TIME_STEP * W3) * whole
            x_next.wait_recv()
            for f in range(5):
                term = c_recv[tick, f // 2].astype(jnp.float32)
                if f % 2:
                    term = pltpu.roll(term, 4, 0)
                add_x(target, f, (TIME_STEP * W3) * term)
                add_x(new, f, term)

    @pl.when(has_up)
    def _():
        for copy in up_copies:
            copy.wait_send()

    for copy in copies:
        copy.wait_send()


def solution(mesh):
    counts = tuple(mesh.shape[name] for name in ("sec", "gx", "gy"))

    def per_device(fields, stored_rates):
        _, _, rows, cols = fields.shape
        halo_x = pltpu.VMEM((TICKS, 5, 8, cols), jnp.float32)
        halo_y = pltpu.VMEM((TICKS, 5, rows // 2, 128), jnp.bfloat16)
        block = (5, rows, cols)
        level_block = pltpu.VMEM((TICKS,) + block, jnp.bfloat16)
        x_terms = pltpu.VMEM((TICKS, 3, 8, cols), jnp.bfloat16)
        return pl.pallas_call(
            lambda *refs: kernel(counts, *refs),
            name="correct",
            out_shape=pltpu.VMEM(fields.shape, fields.dtype),
            in_specs=[pl.BlockSpec(memory_space=pl.ANY)] * 2,
            out_specs=pl.BlockSpec(memory_space=pltpu.VMEM),
            scratch_shapes=[
                pltpu.VMEM((TICKS,) + block, jnp.float32),
                pltpu.VMEM((3,) + block, jnp.bfloat16),
                pltpu.VMEM(block, jnp.float32),
                halo_x,
                halo_x,
                pltpu.VMEM((TICKS, 2, 5, rows // 2, 128), jnp.bfloat16),
                halo_y,
                halo_y,
                level_block,
                level_block,
                x_terms,
                x_terms,
                halo_y,
                halo_y,
                pltpu.VMEM((TICKS,) + block, jnp.float32),
                pltpu.SemaphoreType.DMA((2,)),
                pltpu.SemaphoreType.DMA((TICKS, 2)),
                pltpu.SemaphoreType.DMA((TICKS, 2)),
                pltpu.SemaphoreType.DMA((TICKS, 2)),
                pltpu.SemaphoreType.DMA((TICKS, 2)),
                pltpu.SemaphoreType.DMA((TICKS, 5)),
                pltpu.SemaphoreType.DMA((TICKS, 5)),
                pltpu.SemaphoreType.DMA((TICKS,)),
                pltpu.SemaphoreType.DMA((TICKS,)),
                pltpu.SemaphoreType.DMA((TICKS, 2)),
                pltpu.SemaphoreType.DMA((TICKS, 2)),
            ],
            compiler_params=pltpu.CompilerParams(collective_id=0, has_side_effects=True),
        )(fields, stored_rates)

    return jax.shard_map(
        per_device,
        mesh=mesh,
        in_specs=(P("sec", None, "gx", "gy"), P("sec", None, None, "gx", "gy")),
        out_specs=P("sec", None, "gx", "gy"),
        check_vma=False,
    )
```
